256 devices in a mesh: row: 8 (over z), col: 32 (over y, x, core).
Axes of the slice: x: 4, y: 4, z: 8, core: 2. Of those that a mesh axis runs over, the one named last changes fastest.
Arguments:
- ancestor_inverse: bfloat16 [24576, 24576], P('row', 'col'), may hold values from -6 to 6
- factor_slots: bfloat16 [3, 16384, 512], P(None, ('row', 'col')), may hold values from -0.25 to 0.25
- slot_tiles: int32 [3, 64], replicated, may hold values from -1 to 95, as said below
- parent_factor: bfloat16 [2, 512, 512], replicated, may hold values from -0.25 to 0.25
- diag_inverse: float32 [3, 512, 512], replicated, may hold values from -6 to 6
Outputs:
- inverse_panels: bfloat16 [3, 24576, 512], P(None, ('row', 'col'))
- diag_blocks: float32 [3, 512, 512], replicated
- parent_blocks: float32 [2, 512, 512], replicated
The draws below stay inside these ranges and needn't reach their ends.
Inputs may be any that keep to these rules, and one draw needn't show every extreme that they name: `slot_tiles`: entries b * 2 to b * 2 + 1 of a supernode's row are the slots of column block b: each is -1 (empty) or names a tile from b * 3 to b * 3 + 2, no tile twice; in each supernode some block has all its slots filled. `factor_slots`: rows of an empty slot are not part of the factor.
All inputs are finite; a program needn't handle non-finite values.
Results may differ from the reference program's by a relative error of at most 0.00075.
Values may be sent and summed in bfloat16 or wider, within the bound.
No kernel may reach another device: no remote copies, remote signals or barrier semaphores. Data moves between devices by JAX's collectives and lax.ppermute only.
A program may use at most 128 MiB of HBM per device.

```python
import jax
import jax.numpy as jnp
from jax import lax

TILE = 256
W = 512
TPC = 3
CAP = 2
NODES = 3
BLOCKS = 32
NA = 24576
SLOTS = 64


def draw_slot_tiles(key, part):
    base = jax.random.fold_in(key, 17)
    count_key, forced_key, score_key = jax.random.split(base, 3)
    counts = jax.random.randint(count_key, (NODES, BLOCKS), 0, CAP + 1)
    forced = jax.random.randint(forced_key, (NODES,), 0, BLOCKS)
    counts = jnp.where(jnp.arange(BLOCKS)[None, :] == forced[:, None], CAP, counts)
    scores = jax.random.randint(score_key, (NODES, BLOCKS, TPC), 0, 1 << 20)
    scores = scores * TPC + jnp.arange(TPC)[None, None, :]
    ranking = jnp.argsort(scores, axis=-1)[:, :, :CAP]
    tiles = jnp.arange(BLOCKS)[None, :, None] * TPC + ranking
    filled = jnp.arange(CAP)[None, None, :] < counts[:, :, None]
    result = jnp.where(filled, tiles, -1)
    return result.reshape(NODES, BLOCKS * CAP).astype(jnp.int32)


def raised(drawn, stream_key, source, target, shards_of, factor):
    owner, partner = [(jnp.arange(drawn.shape[axis_at]) // (drawn.shape[axis_at] // shards_of)).reshape([-1 if axis == axis_at else 1 for axis in range(drawn.ndim)]) for axis_at in (source, target)]
    chosen = jax.random.permutation(stream_key, shards_of)[partner]
    strong = (owner == chosen) | (owner == (partner + shards_of // 2) % shards_of)
    return jnp.where(strong, factor * drawn, drawn)


def level_of(stream_key, shape, cuts, smallest, largest):
    def one(position, blocks):
        heights = jax.random.uniform(jax.random.fold_in(jax.random.fold_in(stream_key, 6), position), (blocks,), jnp.float32, smallest / len(cuts), largest / len(cuts))
        return jnp.repeat(jnp.exp(heights), shape[position] // blocks).reshape((-1,) + (1,) * (len(shape) - position - 1))

    loudness = one(*cuts[0])
    for cut in cuts[1:]:
        loudness = loudness * one(*cut)
    return loudness


def noise(key, extent, deviation, most, cuts=(), kind=jnp.bfloat16):
    values = deviation * jax.random.normal(key, extent, jnp.float32)
    if cuts:
        values = values * level_of(key, extent, cuts, -0.22, 0.18)
    return jnp.clip(values, -most, most).astype(kind)


def bell_draw_with(own_key, shape, deviation, limit, cuts, heavy, held_as=jnp.bfloat16):
    values = deviation * jax.random.normal(own_key, shape, jnp.float32)
    if cuts:
        values = values * level_of(own_key, shape, cuts, -0.22, 0.18)
    return jnp.clip(raised(values, jax.random.fold_in(own_key, 3), *heavy), -limit, limit).astype(held_as)


def setup_inputs(seed: int = 0) -> dict:
    splits = jax.random.split(jax.random.key(seed), 6)
    return {
        "ancestor_inverse": noise(splits[0], (NA, NA), 1.0, 6.0, ((0, 8), (1, 32))),
        "factor_slots": bell_draw_with(splits[1], (NODES, SLOTS * TILE, W), (NA // 3) ** -0.5, 0.25, ((1, 256),), (1, 2, 256, 6.0)),
        "slot_tiles": draw_slot_tiles(jax.random.fold_in(splits[5], 71), 0),
        "parent_factor": noise(splits[3], (NODES - 1, W, W), W ** -0.5, 0.25),
        "diag_inverse": noise(splits[4], (NODES, W, W), 1.0, 6.0, (), jnp.float32),
    }


exact_mode = lax.Precision.HIGHEST


def block_panel(ancestor_inverse, factor_node, tiles_node, block_index):
    slot_ids = lax.dynamic_slice_in_dim(tiles_node, block_index * CAP, CAP)
    slot_data = lax.dynamic_slice_in_dim(factor_node, block_index * CAP * TILE, CAP * TILE, 0)
    columns = lax.dynamic_slice_in_dim(ancestor_inverse, block_index * TPC * TILE, TPC * TILE, 1)
    local_tile = slot_ids - block_index * TPC
    pieces = []
    for tile_index in range(TPC):
        chosen = jnp.zeros((TILE, W), jnp.bfloat16)
        for member in range(CAP):
            chosen = jnp.where(local_tile[member] == tile_index, slot_data[member * TILE:(member + 1) * TILE], chosen)
        pieces.append(chosen)
    padded = jnp.concatenate(pieces, axis=0)
    product = jnp.dot(columns, padded, preferred_element_type=jnp.float32)
    return product, padded


def node_panel(ancestor_inverse, factor_node, tiles_node):
    def one_block(total, block_index):
        product, padded = block_panel(ancestor_inverse, factor_node, tiles_node, block_index)
        return total + product, padded

    start_total = jnp.zeros((NA, W), jnp.float32)
    total, padded_all = lax.scan(one_block, start_total, jnp.arange(BLOCKS, dtype=jnp.int32))
    return total, padded_all.reshape(NA, W)


def reference(ancestor_inverse, factor_slots, slot_tiles, parent_factor, diag_inverse):
    panels = []
    diagonals = []
    parents = []
    previous = None
    prev_diag = None
    for node in range(NODES):
        total, padded = node_panel(ancestor_inverse, factor_slots[node], slot_tiles[node])
        dense = padded.astype(jnp.float32)
        column = -total
        if node > 0:
            parent_link = parent_factor[node - 1].astype(jnp.float32)
            column = column - jnp.dot(previous, parent_link, precision=exact_mode)
        first_term = jnp.dot(dense.T, column, precision=exact_mode)
        if node > 0:
            second_term = jnp.dot(previous.T, dense, precision=exact_mode)
            upper = -(second_term + jnp.dot(prev_diag, parent_link, precision=exact_mode))
            diagonal = diag_inverse[node] - first_term - jnp.dot(parent_link.T, upper, precision=exact_mode)
            parents.append(upper)
        else:
            diagonal = diag_inverse[0] - first_term
        panels.append(column.astype(jnp.bfloat16))
        diagonals.append(diagonal)
        previous = column
        prev_diag = diagonal
    return jnp.stack(panels), jnp.stack(diagonals), jnp.stack(parents)
```

```python
import jax
import jax.numpy as jnp
from jax import lax
from jax.sharding import Mesh, PartitionSpec as P

AXES = ("z", "y", "x", "k")
SIZES = (8, 4, 4, 2)
CAP = 2
TPC = 3


exact_mode = lax.Precision.HIGHEST


def number(z, y, x, k):
    return ((z % 8 * 4 + y % 4) * 4 + x % 4) * 2 + k % 2


def hop(value, move):
    pairs = []
    for z in range(8):
        for y in range(4):
            for x in range(4):
                for k in range(2):
                    pairs.append((number(z, y, x, k), number(*move(z, y, x, k))))
    return lax.ppermute(value, AXES, pairs)


def swap_cores(value):
    return hop(value, lambda z, y, x, k: (z, y, x, k + 1))


def step_x(value, by):
    return hop(value, lambda z, y, x, k: (z, y, x + by, k))


def step_y(value, by):
    return hop(value, lambda z, y, x, k: (z, y + by, x, k))


def step_z(value, by):
    return hop(value, lambda z, y, x, k: (z + by, y, x, k))


def to_column(value):
    count = 256
    pairs = [(b * 8 + j, j * 32 + b) for b in range(count // 8) for j in range(8)]
    return lax.ppermute(value, AXES, pairs)


def picked(value, index, axis):
    return lax.dynamic_index_in_dim(value, index, axis, keepdims=False)


def padded_block(slot_data, slot_ids, block_index, tile_rows):
    local_tile = slot_ids - block_index * TPC
    pieces = []
    for tile_index in range(TPC):
        chosen = jnp.zeros((tile_rows, slot_data.shape[1]), slot_data.dtype)
        for member in range(CAP):
            chosen = jnp.where(
                local_tile[member] == tile_index,
                slot_data[member * tile_rows : (member + 1) * tile_rows],
                chosen,
            )
        pieces.append(chosen)
    return jnp.concatenate(pieces, axis=0)


def ring_first(chunks, step):
    half = chunks[2].shape[0] // 2
    low = step(chunks[2][:half], -1)
    high = step(chunks[2][half:], 1)
    return low, high


def ring_second(chunks, low, high, step):
    half = chunks[2].shape[0] // 2
    back = jnp.concatenate([chunks[3][:half] + low, chunks[3][half:]], axis=0)
    ahead = jnp.concatenate([chunks[1][:half], chunks[1][half:] + high], axis=0)
    return chunks[0] + step(back, -1) + step(ahead, 1)


def on_device(ancestor_inverse, factor_slots, slot_tiles, parent_factor, diag_inverse):
    z = lax.axis_index("z")
    y = lax.axis_index("y")
    x = lax.axis_index("x")
    k = lax.axis_index("k")
    block_rows, block_cols = ancestor_inverse.shape
    tile_rows = block_cols // TPC
    node_count, piece_rows, width = factor_slots.shape
    panel_rows = block_rows // 32
    half_width = width // 2
    column_block = (y * 4 + x) * 2 + k
    other_block = (y * 4 + x) * 2 + (1 - k)
    own_block = z * 4 + y

    split_rows = ancestor_inverse.reshape(4, 4, 2, panel_rows, block_cols)
    kept = picked(split_rows, k, 2)
    handed = swap_cores(picked(split_rows, 1 - k, 2))

    first_piece = to_column(factor_slots)
    behind = []
    moving = first_piece
    for _ in range(4):
        moving = step_z(moving, 1)
        behind.append(moving)
    ahead = []
    moving = first_piece
    for _ in range(3):
        moving = step_z(moving, -1)
        ahead.append(moving)
    ring = behind[::-1] + [first_piece] + ahead
    twice = jnp.stack(ring + ring)
    pieces = lax.dynamic_slice_in_dim(twice, (4 - z) % 8, 8, 0)
    other_pieces = swap_cores(pieces)

    group = [factor_slots, step_x(factor_slots, -1), step_x(factor_slots, -2), step_x(factor_slots, -3)]
    group = jnp.stack(group + group)
    group = lax.dynamic_slice_in_dim(group, (4 - x) % 4, 4, 0)
    group_other = swap_cores(group)
    group_even = jnp.where(k == 0, group, group_other)
    group_odd = jnp.where(k == 0, group_other, group)
    group_slots = jnp.stack([group_even, group_odd], axis=1).reshape(8, node_count, piece_rows, width)

    def dense_of(slots, block_index):
        dense = []
        for node in range(node_count):
            ids = lax.dynamic_slice_in_dim(slot_tiles[node], block_index * CAP, CAP)
            rows = slots[:, node].reshape(8 * piece_rows, width)
            dense.append(padded_block(rows, ids, block_index, tile_rows))
        return dense

    own_cols = dense_of(pieces, column_block)
    other_cols = dense_of(other_pieces, other_block)

    def half_columns(lo):
        top = jnp.concatenate([d[:, lo : lo + half_width] for d in own_cols], axis=1)
        bottom = jnp.concatenate([d[:, lo : lo + half_width] for d in other_cols], axis=1)
        return jnp.concatenate([top, bottom], axis=0)

    weights_a = half_columns(0)
    weights_b = half_columns(half_width)
    wide = jnp.concatenate([kept, handed], axis=-1)

    def product(rows, weights):
        flat = rows.reshape(4 * panel_rows, 2 * block_cols)
        return jnp.dot(flat, weights, preferred_element_type=jnp.float32)

    chunks_a = [product(picked(wide, (x + d) % 4, 1), weights_a) for d in range(4)]
    chunks_b = [product(picked(wide, (y + d) % 4, 0), weights_b) for d in range(4)]

    low_a, high_a = ring_first(chunks_a, step_x)
    low_b, high_b = ring_first(chunks_b, step_y)
    sum_a = ring_second(chunks_a, low_a, high_a, step_x)
    sum_b = ring_second(chunks_b, low_b, high_b, step_y)
    sum_a = sum_a.reshape(4, panel_rows, node_count * half_width)
    sum_b = sum_b.reshape(4, panel_rows, node_count * half_width)
    chunks_a = [picked(sum_a, (y + d) % 4, 0) for d in range(4)]
    chunks_b = [picked(sum_b, (x + d) % 4, 0) for d in range(4)]
    low_a, high_a = ring_first(chunks_a, step_y)
    low_b, high_b = ring_first(chunks_b, step_x)
    own_a = ring_second(chunks_a, low_a, high_a, step_y)
    own_b = ring_second(chunks_b, low_b, high_b, step_x)

    links = parent_factor.astype(jnp.float32)
    panels = []
    for node in range(node_count):
        cut = slice(node * half_width, (node + 1) * half_width)
        column = -jnp.concatenate([own_a[:, cut], own_b[:, cut]], axis=1)
        if node > 0:
            column = column - jnp.dot(panels[-1], links[node - 1], precision=exact_mode)
        panels.append(column)

    quarter = width // 4
    spread_cols = jnp.stack(panels, axis=1).reshape(panel_rows, node_count, 4, quarter)
    spread_cols = spread_cols.transpose(2, 1, 0, 3)
    block_cols_x = lax.all_to_all(spread_cols, "x", 0, 0, tiled=True)
    block_panels = [block_cols_x[:, node].reshape(4 * panel_rows, quarter) for node in range(node_count)]
    own_rows = []
    for dense in dense_of(group_slots, own_block):
        mine = picked(dense.reshape(4, 2, panel_rows, width), k, 1)
        own_rows.append(mine.reshape(4 * panel_rows, width).astype(jnp.float32))
    parts = [jnp.dot(own_rows[n].T, block_panels[n], precision=exact_mode) for n in range(node_count)]
    parts += [jnp.dot(own_rows[n].T, block_panels[n - 1], precision=exact_mode) for n in range(1, node_count)]
    sums = jnp.stack(parts)
    count = sums.shape[0]
    sums = sums.reshape(count, 2, half_width, quarter)
    sums = picked(sums, k, 1) + swap_cores(picked(sums, 1 - k, 1))
    strip = half_width // 32
    sums = sums.reshape(count, 32, strip, quarter).transpose(1, 0, 2, 3)
    sums = lax.all_to_all(sums, ("z", "y"), 0, 0, tiled=True)
    sums = jnp.sum(sums, axis=0)
    over_z = lax.all_to_all(jnp.broadcast_to(sums, (8,) + sums.shape), "z", 0, 0, tiled=True)
    over_plane = lax.all_to_all(
        jnp.broadcast_to(over_z, (16,) + over_z.shape), ("y", "x"), 0, 0, tiled=True
    )
    over_other = swap_cores(over_plane)
    both = jnp.stack(
        [jnp.where(k == 0, over_plane, over_other), jnp.where(k == 0, over_other, over_plane)]
    )
    both = both.reshape(2, 4, 4, 8, count, strip, quarter)
    both = both.transpose(4, 0, 3, 1, 5, 2, 6).reshape(count, width, width)

    diagonals = [diag_inverse[0] - both[0]]
    parents = []
    for node in range(1, node_count):
        second = both[node_count + node - 1].T
        upper = -(second + jnp.dot(diagonals[-1], links[node - 1], precision=exact_mode))
        parents.append(upper)
        diagonals.append(
            diag_inverse[node] - both[node] - jnp.dot(links[node - 1].T, upper, precision=exact_mode)
        )
    return (
        jnp.stack(panels).astype(jnp.bfloat16),
        jnp.stack(diagonals),
        jnp.stack(parents),
    )


def solution(mesh):
    grid = Mesh(mesh.devices.reshape(SIZES), AXES)
    placed = (P("z", ("y", "x", "k")), P(None, AXES, None), P(), P(), P())
    return jax.shard_map(
        on_device,
        mesh=grid,
        in_specs=placed,
        out_specs=(P(None, AXES, None), P(), P()),
        check_vma=False,
    )
```

```python
import jax
import jax.numpy as jnp
from jax import lax
from jax.experimental import pallas as pl
from jax.experimental.pallas import tpu as pltpu
from jax.sharding import Mesh, PartitionSpec as P

AXES = ("z", "y", "x", "k")
SIZES = (8, 4, 4, 2)
CAP = 2
TPC = 3


def number(z, y, x, k):
    return ((z % 8 * 4 + y % 4) * 4 + x % 4) * 2 + k % 2


def hop(value, move):
    pairs = []
    for z in range(8):
        for y in range(4):
            for x in range(4):
                for k in range(2):
                    pairs.append((number(z, y, x, k), number(*move(z, y, x, k))))
    return lax.ppermute(value, AXES, pairs)


def swap_cores(value):
    return hop(value, lambda z, y, x, k: (z, y, x, k + 1))


def step_x(value, by):
    return hop(value, lambda z, y, x, k: (z, y, x + by, k))


def step_y(value, by):
    return hop(value, lambda z, y, x, k: (z, y + by, x, k))


def step_z(value, by):
    return hop(value, lambda z, y, x, k: (z + by, y, x, k))


def to_column(value):
    count = 256
    pairs = [(b * 8 + j, j * 32 + b) for b in range(count // 8) for j in range(8)]
    return lax.ppermute(value, AXES, pairs)


def picked(value, index, axis):
    return lax.dynamic_index_in_dim(value, index, axis, keepdims=False)


def three_parts(value):
    high = value.astype(jnp.bfloat16)
    rest = value - high.astype(jnp.float32)
    middle = rest.astype(jnp.bfloat16)
    low = (rest - middle.astype(jnp.float32)).astype(jnp.bfloat16)
    return high, middle, low


def times_exact(value, matrix):
    rows = value.shape[0]
    out = jnp.dot(
        jnp.concatenate(three_parts(value), axis=0), matrix, preferred_element_type=jnp.float32
    )
    return out[:rows] + out[rows : 2 * rows] + out[2 * rows :]


def transposed_times(matrix, value):
    cols = value.shape[1]
    out = lax.dot_general(
        matrix,
        jnp.concatenate(three_parts(value), axis=1),
        (((0,), (0,)), ((), ())),
        preferred_element_type=jnp.float32,
    )
    return out[:, :cols] + out[:, cols : 2 * cols] + out[:, 2 * cols :]


def products(place, tiles, split_rows, handed, ring, other_ring, offsets):
    _, _, _, panel_rows, block_cols = split_rows.shape
    _, node_count, piece_rows, width = ring.shape
    tile_rows = block_cols // TPC
    half = width // 2
    per_slot = tile_rows // piece_rows
    flat_rows = 4 * panel_rows

    def offset_of(i):
        where = jnp.int32(offsets[0])
        for at in range(1, len(offsets)):
            where = jnp.where(i == at, offsets[at], where)
        return where

    def kernel(place, tiles, kept_x, handed_x, kept_y, handed_y, ring, other_ring, out_x, out_y):
        z = place[0]
        own = (place[1] * 4 + place[2]) * 2 + place[3]
        other = (place[1] * 4 + place[2]) * 2 + 1 - place[3]
        for node in range(node_count):
            sums = [None, None]
            for block, slots, column_x, column_y in (
                (own, ring, kept_x, kept_y),
                (other, other_ring, handed_x, handed_y),
            ):
                for member in range(CAP):
                    name = tiles[node, block * CAP + member]
                    tile = jnp.clip(name - block * TPC, 0, TPC - 1)
                    at = pl.ds(pl.multiple_of(tile * tile_rows, tile_rows), tile_rows)
                    rows = jnp.concatenate(
                        [
                            slots[lax.rem(member * per_slot + q - z + 12, 8), node]
                            for q in range(per_slot)
                        ],
                        axis=0,
                    )
                    rows = jnp.where(name >= 0, rows, jnp.zeros_like(rows))
                    left_x = column_x[..., at].reshape(flat_rows, tile_rows)
                    left_y = column_y[..., at].reshape(flat_rows, tile_rows)
                    for side, left in enumerate((left_x, left_y)):
                        term = jnp.dot(
                            left,
                            rows[:, side * half : (side + 1) * half],
                            preferred_element_type=jnp.float32,
                        )
                        sums[side] = term if sums[side] is None else sums[side] + term
            out_x[0, :, node * half : (node + 1) * half] = sums[0]
            out_y[0, :, node * half : (node + 1) * half] = sums[1]

    count = len(offsets)
    out = jax.ShapeDtypeStruct((count, flat_rows, node_count * half), jnp.float32)
    whole = pl.BlockSpec(ring.shape, lambda i, p, t: (0, 0, 0, 0))
    strip = (panel_rows, block_cols)
    return pl.pallas_call(
        kernel,
        grid_spec=pltpu.PrefetchScalarGridSpec(
            num_scalar_prefetch=2,
            grid=(count,),
            in_specs=[
                pl.BlockSpec(
                    (4, 1, 1) + strip,
                    lambda i, p, t: (0, lax.rem(p[2] + offset_of(i), 4), p[3], 0, 0),
                ),
                pl.BlockSpec(
                    (4, 1) + strip, lambda i, p, t: (0, lax.rem(p[2] + offset_of(i), 4), 0, 0)
                ),
                pl.BlockSpec(
                    (1, 4, 1) + strip,
                    lambda i, p, t: (lax.rem(p[1] + offset_of(i), 4), 0, p[3], 0, 0),
                ),
                pl.BlockSpec(
                    (1, 4) + strip, lambda i, p, t: (lax.rem(p[1] + offset_of(i), 4), 0, 0, 0)
                ),
                whole,
                whole,
            ],
            out_specs=[pl.BlockSpec((1,) + out.shape[1:], lambda i, p, t: (i, 0, 0))] * 2,
        ),
        out_shape=[out, out],
        name="products" + str(count),
    )(place, tiles, split_rows, handed, split_rows, handed, ring, other_ring)


def chain(own_x, own_y, links, node_count):
    panel_rows = own_x.shape[0]
    half = own_x.shape[1] // node_count
    width = 2 * half
    quarter = width // 4

    def kernel(own_x, own_y, links, panels, spread):
        previous = None
        for node in range(node_count):
            cut = slice(node * half, (node + 1) * half)
            column = -jnp.concatenate([own_x[:, cut], own_y[:, cut]], axis=1)
            if node > 0:
                column = column - times_exact(previous, links[node - 1])
            panels[node] = column.astype(jnp.bfloat16)
            for part in range(4):
                spread[part, node] = column[:, part * quarter : (part + 1) * quarter]
            previous = column

    return pl.pallas_call(
        kernel,
        out_shape=[
            jax.ShapeDtypeStruct((node_count, panel_rows, width), jnp.bfloat16),
            jax.ShapeDtypeStruct((4, node_count, panel_rows, quarter), jnp.float32),
        ],
        name="chain",
    )(own_x, own_y, links)


def contraction(place, tiles, block_panels, group):
    _, node_count, panel_rows, quarter = block_panels.shape
    _, _, _, piece_rows, width = group.shape
    half = width // 2
    granule = panel_rows // 3
    per_tile = piece_rows * 8 // CAP // granule
    per_piece = piece_rows // granule
    count = 2 * node_count - 1
    strip = half // 32

    def kernel(place, tiles, block_panels, group, keep, send, sums):
        x = place[2]
        k = place[3]
        block = place[0] * 4 + place[1]
        parts = []
        for node in range(node_count):
            first = tiles[node, block * CAP] - block * TPC
            second = tiles[node, block * CAP + 1] - block * TPC
            rows = []
            for part in range(4):
                for i in range(3):
                    at = 3 * (2 * part + k) + i
                    tile = at // per_tile
                    inner = at - tile * per_tile
                    in_second = second == tile
                    live = jnp.logical_or(first == tile, in_second)
                    piece = jnp.where(in_second, 8 // CAP, 0) + inner // per_piece
                    start = pl.multiple_of(lax.rem(inner, per_piece) * granule, granule)
                    side = jnp.where(lax.rem(piece, 2) == k, 0, 1)
                    along = lax.rem(piece // 2 - x + 4, 4)
                    value = group[side, along, node, pl.ds(start, granule), :]
                    rows.append(jnp.where(live, value, jnp.zeros_like(value)))
            dense = jnp.concatenate(rows, axis=0)
            parts.append(three_parts(block_panels[:, node].reshape(4 * panel_rows, quarter)))
            right = parts[node] if node == 0 else parts[node] + parts[node - 1]
            out = lax.dot_general(
                dense,
                jnp.concatenate(right, axis=1),
                (((0,), (0,)), ((), ())),
                preferred_element_type=jnp.float32,
            )
            cols = [out[:, i * quarter : (i + 1) * quarter] for i in range(len(right))]
            sums[node] = cols[0] + cols[1] + cols[2]
            if node > 0:
                sums[node_count + node - 1] = cols[3] + cols[4] + cols[5]
        mine = pl.multiple_of(k * half, half)
        theirs = pl.multiple_of((1 - k) * half, half)
        for i in range(count):
            keep[:, i] = sums[i, pl.ds(mine, half), :].reshape(32, strip, quarter)
            send[:, i] = sums[i, pl.ds(theirs, half), :].reshape(32, strip, quarter)

    out = jax.ShapeDtypeStruct((32, count, strip, quarter), jnp.float32)
    vmem = pl.BlockSpec(memory_space=pltpu.VMEM)
    smem = pl.BlockSpec(memory_space=pltpu.SMEM)
    return pl.pallas_call(
        kernel,
        in_specs=[smem, smem, vmem, vmem],
        out_specs=[vmem, vmem],
        out_shape=[out, out],
        scratch_shapes=[pltpu.VMEM((count, width, quarter), jnp.float32)],
        name="contraction",
    )(place, tiles, block_panels, group)


def tail(place, plane, other, links, diag_inverse):
    _, _, count, strip, quarter = plane.shape
    node_count, width, _ = diag_inverse.shape

    def kernel(place, plane, other, links, diag_inverse, diagonals, parents, sums):
        k = place[3]
        for source, side in ((plane, k), (other, 1 - k)):
            for y in range(4):
                for x in range(4):
                    for i in range(count):
                        sums[i, side, :, y, :, x * quarter : (x + 1) * quarter] = source[
                            y * 4 + x, :, i
                        ]
        total = [sums[i].reshape(width, width) for i in range(count)]
        diagonal = diag_inverse[0] - total[0]
        diagonals[0] = diagonal
        for node in range(1, node_count):
            link = links[node - 1]
            upper = -(total[node_count + node - 1].T + times_exact(diagonal, link))
            parents[node - 1] = upper
            diagonal = diag_inverse[node] - total[node] - transposed_times(link, upper)
            diagonals[node] = diagonal

    vmem = pl.BlockSpec(memory_space=pltpu.VMEM)
    smem = pl.BlockSpec(memory_space=pltpu.SMEM)
    return pl.pallas_call(
        kernel,
        in_specs=[smem, vmem, vmem, vmem, vmem],
        out_specs=[vmem, vmem],
        out_shape=[
            jax.ShapeDtypeStruct((node_count, width, width), jnp.float32),
            jax.ShapeDtypeStruct((node_count - 1, width, width), jnp.float32),
        ],
        scratch_shapes=[pltpu.VMEM((count, 2, 8, 4, strip, width), jnp.float32)],
        name="tail",
    )(place, plane, other, links, diag_inverse)


def ring_first(middle, step):
    half = middle.shape[0] // 2
    return step(middle[:half], -1), step(middle[half:], 1)


def ring_second(last, first, own, low, high, step):
    half = last.shape[0] // 2
    back = jnp.concatenate([last[:half] + low, last[half:]], axis=0)
    ahead = jnp.concatenate([first[:half], first[half:] + high], axis=0)
    return own + step(back, -1) + step(ahead, 1)


def on_device(ancestor_inverse, factor_slots, slot_tiles, parent_factor, diag_inverse):
    z = lax.axis_index("z")
    y = lax.axis_index("y")
    x = lax.axis_index("x")
    k = lax.axis_index("k")
    place = jnp.stack([z, y, x, k]).astype(jnp.int32)
    block_rows, block_cols = ancestor_inverse.shape
    node_count, piece_rows, width = factor_slots.shape
    panel_rows = block_rows // 32
    half = width // 2

    first_piece = to_column(factor_slots)

    split_rows = ancestor_inverse.reshape(4, 4, 2, panel_rows, block_cols)
    handed = swap_cores(picked(split_rows, 1 - k, 2))

    behind = []
    moving = first_piece
    for _ in range(4):
        moving = step_z(moving, 1)
        behind.append(moving)
    ahead = []
    moving = first_piece
    for _ in range(3):
        moving = step_z(moving, -1)
        ahead.append(moving)
    ring = jnp.stack(behind[::-1] + [first_piece] + ahead)
    other_ring = swap_cores(ring)

    near = jnp.stack([factor_slots] + [step_x(factor_slots, -i) for i in range(1, 4)])
    group = jnp.stack([near, swap_cores(near)])

    opposite_x, opposite_y = products(
        place, slot_tiles, split_rows, handed, ring, other_ring, (2,)
    )
    rest_x, rest_y = products(
        place, slot_tiles, split_rows, handed, ring, other_ring, (3, 1, 0)
    )
    low_a, high_a = ring_first(opposite_x[0], step_x)
    low_b, high_b = ring_first(opposite_y[0], step_y)
    sum_a = ring_second(rest_x[0], rest_x[1], rest_x[2], low_a, high_a, step_x)
    sum_b = ring_second(rest_y[0], rest_y[1], rest_y[2], low_b, high_b, step_y)
    sum_a = sum_a.reshape(4, panel_rows, node_count * half)
    sum_b = sum_b.reshape(4, panel_rows, node_count * half)
    a = [picked(sum_a, (y + d) % 4, 0) for d in range(4)]
    b = [picked(sum_b, (x + d) % 4, 0) for d in range(4)]
    low_a, high_a = ring_first(a[2], step_y)
    low_b, high_b = ring_first(b[2], step_x)
    own_a = ring_second(a[3], a[1], a[0], low_a, high_a, step_y)
    own_b = ring_second(b[3], b[1], b[0], low_b, high_b, step_x)

    panels, spread = chain(own_a, own_b, parent_factor, node_count)

    block_panels = lax.all_to_all(spread, "x", 0, 0, tiled=True)
    keep, send = contraction(place, slot_tiles, block_panels, group)
    sums = lax.all_to_all(keep + swap_cores(send), ("z", "y"), 0, 0, tiled=True)
    sums = jnp.sum(sums, axis=0)
    over_z = lax.all_to_all(jnp.broadcast_to(sums, (8,) + sums.shape), "z", 0, 0, tiled=True)
    plane = lax.all_to_all(
        jnp.broadcast_to(over_z, (16,) + over_z.shape), ("y", "x"), 0, 0, tiled=True
    )
    diagonals, parents = tail(place, plane, swap_cores(plane), parent_factor, diag_inverse)
    return panels, diagonals, parents


def solution(mesh):
    grid = Mesh(mesh.devices.reshape(SIZES), AXES)
    placed = (P("z", ("y", "x", "k")), P(None, AXES, None), P(), P(), P())
    return jax.shard_map(
        on_device,
        mesh=grid,
        in_specs=placed,
        out_specs=(P(None, AXES, None), P(), P()),
        check_vma=False,
    )
```

```python
import jax
import jax.numpy as jnp
from jax import lax
from jax.experimental import pallas as pl
from jax.experimental.pallas import tpu as pltpu
from jax.sharding import Mesh, PartitionSpec as P

AXES = ("z", "y", "x", "k")
SIZES = (8, 4, 4, 2)
CAP = 2
TPC = 3


def number(z, y, x, k):
    return ((z % 8 * 4 + y % 4) * 4 + x % 4) * 2 + k % 2


def hop(value, move):
    pairs = []
    for z in range(8):
        for y in range(4):
            for x in range(4):
                for k in range(2):
                    pairs.append((number(z, y, x, k), number(*move(z, y, x, k))))
    return lax.ppermute(value, AXES, pairs)


def swap_cores(value):
    return hop(value, lambda z, y, x, k: (z, y, x, k + 1))


def step_x(value, by):
    return hop(value, lambda z, y, x, k: (z, y, x + by, k))


def step_first(value, by):
    return hop(value, lambda z, y, x, k: (z, y + by * k, x + by * (1 - k), k))


def step_second(value, by):
    return hop(value, lambda z, y, x, k: (z, y + by * (1 - k), x + by * k, k))


def step_z(value, by):
    return hop(value, lambda z, y, x, k: (z + by, y, x, k))


def to_column(value):
    count = 256
    pairs = [(b * 8 + j, j * 32 + b) for b in range(count // 8) for j in range(8)]
    return lax.ppermute(value, AXES, pairs)


def picked(value, index, axis):
    return lax.dynamic_index_in_dim(value, index, axis, keepdims=False)


def three_parts(value):
    high = value.astype(jnp.bfloat16)
    rest = value - high.astype(jnp.float32)
    middle = rest.astype(jnp.bfloat16)
    low = (rest - middle.astype(jnp.float32)).astype(jnp.bfloat16)
    return high, middle, low


def times_exact(value, matrix):
    rows = value.shape[0]
    out = jnp.dot(
        jnp.concatenate(three_parts(value), axis=0), matrix, preferred_element_type=jnp.float32
    )
    return out[:rows] + out[rows : 2 * rows] + out[2 * rows :]


def transposed_times(matrix, value):
    cols = value.shape[1]
    out = lax.dot_general(
        matrix,
        jnp.concatenate(three_parts(value), axis=1),
        (((0,), (0,)), ((), ())),
        preferred_element_type=jnp.float32,
    )
    return out[:, :cols] + out[:, cols : 2 * cols] + out[:, 2 * cols :]


def stacked(pieces):
    count = len(pieces)

    def kernel(*refs):
        for i in range(count):
            refs[count][i] = refs[i][...]

    return pl.pallas_call(
        kernel,
        out_shape=jax.ShapeDtypeStruct((count,) + pieces[0].shape, pieces[0].dtype),
        name="stacked" + str(count),
    )(*pieces)


def products(place, tiles, split_rows, handed, own_pieces, other_groups, offset):
    _, _, _, panel_rows, block_cols = split_rows.shape
    node_count, piece_rows, width = own_pieces[0].shape
    tile_rows = block_cols // TPC
    half = width // 2
    per_slot = tile_rows // piece_rows
    flat_rows = 4 * panel_rows
    other_arrays = [array for _, array in other_groups]

    def kernel(place, tiles, *refs):
        kept = refs[0:4]
        given = refs[4:8]
        pieces = refs[8:16]
        others = refs[16 : 16 + len(other_arrays)]
        low, high, slots = refs[16 + len(other_arrays) :]
        node = pl.program_id(0)
        z = place[0]
        own = (place[1] * 4 + place[2]) * 2 + place[3]
        other = (place[1] * 4 + place[2]) * 2 + 1 - place[3]
        for i in range(8):
            slots[0, lax.rem(z + i + 4, 8)] = pieces[i][0]
        for (spots, _), ref in zip(other_groups, others):
            for at, i in enumerate(spots):
                slots[1, lax.rem(z + i + 4, 8)] = ref[at, 0]
        sums = [None, None]
        for side, block, parts in ((0, own, kept), (1, other, given)):
            for member in range(CAP):
                name = tiles[node, block * CAP + member]
                tile = jnp.clip(name - block * TPC, 0, TPC - 1)
                at = pl.ds(pl.multiple_of(tile * tile_rows, tile_rows), tile_rows)
                rows = slots[side, member * per_slot : (member + 1) * per_slot]
                rows = rows.reshape(tile_rows, width)
                rows = jnp.where(name >= 0, rows, jnp.zeros_like(rows))
                left = jnp.concatenate(
                    [part[..., at].reshape(panel_rows, tile_rows) for part in parts], axis=0
                )
                for i in range(2):
                    term = jnp.dot(
                        left, rows[:, i * half : (i + 1) * half], preferred_element_type=jnp.float32
                    )
                    sums[i] = term if sums[i] is None else sums[i] + term
        low[...] = sums[0].reshape(4, panel_rows, half)
        high[...] = sums[1].reshape(4, panel_rows, half)

    def at_chip(j, p):
        along_y = jnp.where(p[3] == 0, j, lax.rem(p[1] + offset, 4))
        along_x = jnp.where(p[3] == 0, lax.rem(p[2] + offset, 4), j)
        return along_y, along_x

    def kept_at(j):
        return lambda i, p, t: at_chip(j, p) + (p[3], 0, 0)

    def given_at(j):
        return lambda i, p, t: at_chip(j, p) + (0, 0)

    strip = (panel_rows, block_cols)
    out = jax.ShapeDtypeStruct((4, panel_rows, node_count * half), jnp.float32)
    return pl.pallas_call(
        kernel,
        grid_spec=pltpu.PrefetchScalarGridSpec(
            num_scalar_prefetch=2,
            grid=(node_count,),
            in_specs=[pl.BlockSpec((1, 1, 1) + strip, kept_at(j)) for j in range(4)]
            + [pl.BlockSpec((1, 1) + strip, given_at(j)) for j in range(4)]
            + [pl.BlockSpec((1, piece_rows, width), lambda i, p, t: (i, 0, 0))] * 8
            + [
                pl.BlockSpec(
                    (array.shape[0], 1, piece_rows, width), lambda i, p, t: (0, i, 0, 0)
                )
                for array in other_arrays
            ],
            out_specs=[pl.BlockSpec((4, panel_rows, half), lambda i, p, t: (0, 0, i))] * 2,
            scratch_shapes=[pltpu.VMEM((2, 8, piece_rows, width), jnp.bfloat16)],
        ),
        out_shape=[out, out],
        name="products" + str(offset),
    )(place, tiles, *[split_rows] * 4, *[handed] * 4, *own_pieces, *other_arrays)


def regroup(place, low, high):
    _, panel_rows, cols = low[0].shape

    def kernel(place, *refs):
        here = jnp.where(place[3] == 0, place[1], place[2])
        for group in range(2):
            first, second, third = refs[3 * group : 3 * group + 3]
            for e in range(4):
                at = lax.rem(here + e, 4)
                refs[6 + 4 * group + e][...] = first[at] + second[at] + third[at]

    vmem = pl.BlockSpec(memory_space=pltpu.VMEM)
    smem = pl.BlockSpec(memory_space=pltpu.SMEM)
    out = jax.ShapeDtypeStruct((panel_rows, cols), jnp.float32)
    outs = pl.pallas_call(
        kernel,
        in_specs=[smem] + [vmem] * 6,
        out_specs=[vmem] * 8,
        out_shape=[out] * 8,
        name="regroup",
    )(place, *low, *high)
    return outs[:4], outs[4:]


def chain(place, low, high, links, node_count):
    panel_rows = low[0].shape[0]
    half = low[0].shape[1] // node_count
    width = 2 * half
    quarter = width // 4

    def kernel(place, *refs):
        low = refs[0:3]
        high = refs[3:6]
        links, panels = refs[6:8]
        spread = refs[8:12]
        columns = refs[12]
        previous = None
        for node in range(node_count):
            cut = slice(node * half, (node + 1) * half)
            column = -jnp.concatenate(
                [
                    low[0][:, cut] + low[1][:, cut] + low[2][:, cut],
                    high[0][:, cut] + high[1][:, cut] + high[2][:, cut],
                ],
                axis=1,
            )
            if node > 0:
                column = column - times_exact(previous, links[node - 1])
            panels[node] = column.astype(jnp.bfloat16)
            columns[node] = column
            previous = column
        for d in range(4):
            start = pl.multiple_of(lax.rem(place[2] + d, 4) * quarter, quarter)
            spread[d][...] = columns[:, :, pl.ds(start, quarter)]

    vmem = pl.BlockSpec(memory_space=pltpu.VMEM)
    smem = pl.BlockSpec(memory_space=pltpu.SMEM)
    part = jax.ShapeDtypeStruct((node_count, panel_rows, quarter), jnp.float32)
    outs = pl.pallas_call(
        kernel,
        in_specs=[smem] + [vmem] * 7,
        out_specs=[vmem] * 5,
        out_shape=[jax.ShapeDtypeStruct((node_count, panel_rows, width), jnp.bfloat16)] + [part] * 4,
        scratch_shapes=[pltpu.VMEM((node_count, panel_rows, width), jnp.float32)],
        name="chain",
    )(place, *low, *high, links)
    return outs[0], outs[1:]


def contraction(place, tiles, block_panels, group):
    node_count, panel_rows, quarter = block_panels[0].shape
    _, _, _, piece_rows, width = group.shape
    half = width // 2
    granule = panel_rows // 3
    per_tile = piece_rows * 8 // CAP // granule
    per_piece = piece_rows // granule
    count = 2 * node_count - 1
    strip = half // 32

    def kernel(place, tiles, *refs):
        block_panels = refs[:4]
        group, keep, send, sums = refs[4:]
        x = place[2]
        k = place[3]
        block = place[0] * 4 + place[1]
        parts = []
        for node in range(node_count):
            first = tiles[node, block * CAP] - block * TPC
            second = tiles[node, block * CAP + 1] - block * TPC
            rows = []
            for d in range(4):
                part = lax.rem(x - d + 4, 4)
                for i in range(3):
                    at = 3 * (2 * part + k) + i
                    tile = at // per_tile
                    inner = at - tile * per_tile
                    in_second = second == tile
                    live = jnp.logical_or(first == tile, in_second)
                    piece = jnp.where(in_second, 8 // CAP, 0) + inner // per_piece
                    start = pl.multiple_of(lax.rem(inner, per_piece) * granule, granule)
                    side = jnp.where(lax.rem(piece, 2) == k, 0, 1)
                    along = lax.rem(piece // 2 - x + 4, 4)
                    value = group[side, along, node, pl.ds(start, granule), :]
                    rows.append(jnp.where(live, value, jnp.zeros_like(value)))
            dense = jnp.concatenate(rows, axis=0)
            parts.append(three_parts(jnp.concatenate([p[node] for p in block_panels], axis=0)))
            right = parts[node] if node == 0 else parts[node] + parts[node - 1]
            out = lax.dot_general(
                dense,
                jnp.concatenate(right, axis=1),
                (((0,), (0,)), ((), ())),
                preferred_element_type=jnp.float32,
            )
            cols = [out[:, i * quarter : (i + 1) * quarter] for i in range(len(right))]
            sums[node] = cols[0] + cols[1] + cols[2]
            if node > 0:
                sums[node_count + node - 1] = cols[3] + cols[4] + cols[5]
        mine = pl.multiple_of(k * half, half)
        theirs = pl.multiple_of((1 - k) * half, half)
        for i in range(count):
            keep[:, i] = sums[i, pl.ds(mine, half), :].reshape(32, strip, quarter)
            send[:, i] = sums[i, pl.ds(theirs, half), :].reshape(32, strip, quarter)

    out = jax.ShapeDtypeStruct((32, count, strip, quarter), jnp.float32)
    vmem = pl.BlockSpec(memory_space=pltpu.VMEM)
    smem = pl.BlockSpec(memory_space=pltpu.SMEM)
    return pl.pallas_call(
        kernel,
        in_specs=[smem, smem] + [vmem] * 5,
        out_specs=[vmem, vmem],
        out_shape=[out, out],
        scratch_shapes=[pltpu.VMEM((count, width, quarter), jnp.float32)],
        name="contraction",
    )(place, tiles, *block_panels, group)


def tail(place, plane, other, links, diag_inverse):
    _, _, count, strip, quarter = plane.shape
    node_count, width, _ = diag_inverse.shape

    def kernel(place, plane, other, links, diag_inverse, diagonals, parents, sums):
        k = place[3]
        for source, side in ((plane, k), (other, 1 - k)):
            for y in range(4):
                for x in range(4):
                    for i in range(count):
                        sums[i, side, :, y, :, x * quarter : (x + 1) * quarter] = source[
                            y * 4 + x, :, i
                        ]
        total = [sums[i].reshape(width, width) for i in range(count)]
        diagonal = diag_inverse[0] - total[0]
        diagonals[0] = diagonal
        for node in range(1, node_count):
            link = links[node - 1]
            upper = -(total[node_count + node - 1].T + times_exact(diagonal, link))
            parents[node - 1] = upper
            diagonal = diag_inverse[node] - total[node] - transposed_times(link, upper)
            diagonals[node] = diagonal

    vmem = pl.BlockSpec(memory_space=pltpu.VMEM)
    smem = pl.BlockSpec(memory_space=pltpu.SMEM)
    return pl.pallas_call(
        kernel,
        in_specs=[smem, vmem, vmem, vmem, vmem],
        out_specs=[vmem, vmem],
        out_shape=[
            jax.ShapeDtypeStruct((node_count, width, width), jnp.float32),
            jax.ShapeDtypeStruct((node_count - 1, width, width), jnp.float32),
        ],
        scratch_shapes=[pltpu.VMEM((count, 2, 8, 4, strip, width), jnp.float32)],
        name="tail",
    )(place, plane, other, links, diag_inverse)


def ring_sum(own, behind, middle, ahead, step):
    far_low = step(middle[0], -1)
    far_high = step(middle[1], 1)
    raw_low = step(ahead[0], 1)
    raw_high = step(behind[1], -1)
    low = (own[0], raw_low, step(behind[0] + far_low, -1))
    high = (own[1], raw_high, step(ahead[1] + far_high, 1))
    return low, high


def on_device(ancestor_inverse, factor_slots, slot_tiles, parent_factor, diag_inverse):
    z = lax.axis_index("z")
    y = lax.axis_index("y")
    x = lax.axis_index("x")
    k = lax.axis_index("k")
    place = jnp.stack([z, y, x, k]).astype(jnp.int32)
    block_rows, block_cols = ancestor_inverse.shape
    node_count, piece_rows, width = factor_slots.shape
    panel_rows = block_rows // 32

    split_rows = ancestor_inverse.reshape(4, 4, 2, panel_rows, block_cols)
    leaving = picked(split_rows, 1 - k, 2)
    first_piece, leaving = lax.optimization_barrier((to_column(factor_slots), leaving))
    handed = swap_cores(leaving)

    behind = []
    ahead = []
    moving_up = moving_down = first_piece
    for i in range(4):
        moving_up = step_z(moving_up, 1)
        behind.append(moving_up)
        if i < 3:
            moving_down = step_z(moving_down, -1)
            ahead.append(moving_down)
    own_pieces = behind[::-1] + [first_piece] + ahead
    early = swap_cores(stacked(own_pieces[2:7]))
    late = swap_cores(stacked([own_pieces[0], own_pieces[1], own_pieces[7]]))
    other_groups = [((2, 3, 4, 5, 6), early), ((0, 1, 7), late)]

    near = stacked([factor_slots] + [step_x(factor_slots, -i) for i in range(1, 4)])
    group = jnp.stack([near, swap_cores(near)])

    middle, behind_share, ahead_share, own_share = [
        products(place, slot_tiles, split_rows, handed, own_pieces, other_groups, d)
        for d in (2, 3, 1, 0)
    ]
    low, high = ring_sum(own_share, behind_share, middle, ahead_share, step_first)
    low, high = regroup(place, low, high)
    low, high = ring_sum(
        (low[0], high[0]), (low[3], high[3]), (low[2], high[2]), (low[1], high[1]), step_second
    )
    panels, spread = chain(place, low, high, parent_factor, node_count)

    block_panels = [spread[0]] + [step_x(spread[d], d) for d in range(1, 4)]
    keep, send = contraction(place, slot_tiles, block_panels, group)
    sums = lax.all_to_all(keep + swap_cores(send), ("z", "y"), 0, 0, tiled=True)
    sums = jnp.sum(sums, axis=0)
    over_z = lax.all_to_all(jnp.broadcast_to(sums, (8,) + sums.shape), "z", 0, 0, tiled=True)
    plane = lax.all_to_all(
        jnp.broadcast_to(over_z, (16,) + over_z.shape), ("y", "x"), 0, 0, tiled=True
    )
    diagonals, parents = tail(place, plane, swap_cores(plane), parent_factor, diag_inverse)
    return panels, diagonals, parents


def solution(mesh):
    grid = Mesh(mesh.devices.reshape(SIZES), AXES)
    placed = (P("z", ("y", "x", "k")), P(None, AXES, None), P(), P(), P())
    return jax.shard_map(
        on_device,
        mesh=grid,
        in_specs=placed,
        out_specs=(P(None, AXES, None), P(), P()),
        check_vma=False,
    )
```

```python
import jax
import jax.numpy as jnp
from jax import lax
from jax.experimental import pallas as pl
from jax.experimental.pallas import tpu as pltpu
from jax.sharding import Mesh, PartitionSpec as P

AXES = ("z", "y", "x", "k")
SIZES = (8, 4, 4, 2)
CAP = 2
TPC = 3


def number(z, y, x, k):
    return ((z % 8 * 4 + y % 4) * 4 + x % 4) * 2 + k % 2


def hop(value, move):
    pairs = []
    for z in range(8):
        for y in range(4):
            for x in range(4):
                for k in range(2):
                    pairs.append((number(z, y, x, k), number(*move(z, y, x, k))))
    return lax.ppermute(value, AXES, pairs)


def swap_cores(value):
    return hop(value, lambda z, y, x, k: (z, y, x, k + 1))


def step_x(value, by):
    return hop(value, lambda z, y, x, k: (z, y, x + by, k))


def step_first(value, by):
    return hop(value, lambda z, y, x, k: (z, y + by * k, x + by * (1 - k), k))


def step_second(value, by):
    return hop(value, lambda z, y, x, k: (z, y + by * (1 - k), x + by * k, k))


def step_z(value, by):
    return hop(value, lambda z, y, x, k: (z + by, y, x, k))


def to_column(value):
    count = 256
    pairs = [(b * 8 + j, j * 32 + b) for b in range(count // 8) for j in range(8)]
    return lax.ppermute(value, AXES, pairs)


def after(value, other):
    return lax.optimization_barrier((value, other))[0]


def picked(value, index, axis):
    return lax.dynamic_index_in_dim(value, index, axis, keepdims=False)


def three_parts(value):
    high = value.astype(jnp.bfloat16)
    rest = value - high.astype(jnp.float32)
    middle = rest.astype(jnp.bfloat16)
    low = (rest - middle.astype(jnp.float32)).astype(jnp.bfloat16)
    return high, middle, low


def times_exact(value, matrix):
    rows = value.shape[0]
    out = jnp.dot(
        jnp.concatenate(three_parts(value), axis=0), matrix, preferred_element_type=jnp.float32
    )
    return out[:rows] + out[rows : 2 * rows] + out[2 * rows :]


def transposed_times(matrix, value):
    cols = value.shape[1]
    out = lax.dot_general(
        matrix,
        jnp.concatenate(three_parts(value), axis=1),
        (((0,), (0,)), ((), ())),
        preferred_element_type=jnp.float32,
    )
    return out[:, :cols] + out[:, cols : 2 * cols] + out[:, 2 * cols :]


def stacked(pieces):
    count = len(pieces)

    def kernel(*refs):
        for i in range(count):
            refs[count][i] = refs[i][...]

    return pl.pallas_call(
        kernel,
        out_shape=jax.ShapeDtypeStruct((count,) + pieces[0].shape, pieces[0].dtype),
        name="stacked" + str(count),
    )(*pieces)


def products(place, tiles, split_rows, handed, own_pieces, other_groups, offsets, base):
    _, _, _, panel_rows, block_cols = split_rows.shape
    node_count, piece_rows, width = own_pieces[0].shape
    tile_rows = block_cols // TPC
    half = width // 2
    per_slot = tile_rows // piece_rows
    flat_rows = 4 * panel_rows
    other_arrays = [array for _, array in other_groups]
    spans = len(offsets)

    def offset_of(i):
        where = jnp.int32(offsets[0])
        for at in range(1, spans):
            where = jnp.where(i == at, offsets[at], where)
        return where

    def kernel(place, tiles, *refs):
        kept = refs[0:4]
        given = refs[4:8]
        pieces = refs[8:16]
        others = refs[16 : 16 + len(other_arrays)]
        outs = refs[16 + len(other_arrays) : -1]
        slots = refs[-1]
        node = pl.program_id(1)
        z = place[0]
        own = (place[1] * 4 + place[2]) * 2 + place[3]
        other = (place[1] * 4 + place[2]) * 2 + 1 - place[3]
        for i in range(8):
            slots[0, lax.rem(z + i + 4, 8)] = pieces[i][0]
        for (spots, _), ref in zip(other_groups, others):
            for at, i in enumerate(spots):
                slots[1, lax.rem(z + i + 4, 8)] = ref[at, 0]
        sums = [None, None]
        for side, block, parts in ((0, own, kept), (1, other, given)):
            for member in range(CAP):
                name = tiles[base + node, block * CAP + member]
                tile = jnp.clip(name - block * TPC, 0, TPC - 1)
                at = pl.ds(pl.multiple_of(tile * tile_rows, tile_rows), tile_rows)
                rows = slots[side, member * per_slot : (member + 1) * per_slot]
                rows = rows.reshape(tile_rows, width)
                rows = jnp.where(name >= 0, rows, jnp.zeros_like(rows))
                left = jnp.concatenate(
                    [part[..., at].reshape(panel_rows, tile_rows) for part in parts], axis=0
                )
                for i in range(2):
                    term = jnp.dot(
                        left, rows[:, i * half : (i + 1) * half], preferred_element_type=jnp.float32
                    )
                    sums[i] = term if sums[i] is None else sums[i] + term
        for at in range(spans):

            @pl.when(pl.program_id(0) == at)
            def _():
                outs[2 * at][...] = sums[0].reshape(4, panel_rows, half)
                outs[2 * at + 1][...] = sums[1].reshape(4, panel_rows, half)

    def at_chip(j, d, p):
        along_y = jnp.where(p[3] == 0, j, lax.rem(p[1] + offset_of(d), 4))
        along_x = jnp.where(p[3] == 0, lax.rem(p[2] + offset_of(d), 4), j)
        return along_y, along_x

    def kept_at(j):
        return lambda d, i, p, t: at_chip(j, d, p) + (p[3], 0, 0)

    def given_at(j):
        return lambda d, i, p, t: at_chip(j, d, p) + (0, 0)

    def out_at(at):
        return lambda d, i, p, t: (
            0,
            0,
            jnp.where(d == at, i, jnp.where(d < at, 0, node_count - 1)),
        )

    strip = (panel_rows, block_cols)
    out = jax.ShapeDtypeStruct((4, panel_rows, node_count * half), jnp.float32)
    return pl.pallas_call(
        kernel,
        grid_spec=pltpu.PrefetchScalarGridSpec(
            num_scalar_prefetch=2,
            grid=(spans, node_count),
            in_specs=[pl.BlockSpec((1, 1, 1) + strip, kept_at(j)) for j in range(4)]
            + [pl.BlockSpec((1, 1) + strip, given_at(j)) for j in range(4)]
            + [pl.BlockSpec((1, piece_rows, width), lambda d, i, p, t: (i, 0, 0))] * 8
            + [
                pl.BlockSpec(
                    (array.shape[0], 1, piece_rows, width), lambda d, i, p, t: (0, i, 0, 0)
                )
                for array in other_arrays
            ],
            out_specs=[
                pl.BlockSpec((4, panel_rows, half), out_at(at)) for at in range(spans) for _ in range(2)
            ],
            scratch_shapes=[pltpu.VMEM((2, 8, piece_rows, width), jnp.bfloat16)],
        ),
        out_shape=[out] * (2 * spans),
        name="products" + str(base) + str(spans),
    )(place, tiles, *[split_rows] * 4, *[handed] * 4, *own_pieces, *other_arrays)


def regroup(place, low, high):
    _, panel_rows, cols = low[0].shape

    def kernel(place, *refs):
        here = jnp.where(place[3] == 0, place[1], place[2])
        for group in range(2):
            first, second, third = refs[3 * group : 3 * group + 3]
            for e in range(4):
                at = lax.rem(here + e, 4)
                refs[6 + 4 * group + e][...] = first[at] + second[at] + third[at]

    vmem = pl.BlockSpec(memory_space=pltpu.VMEM)
    smem = pl.BlockSpec(memory_space=pltpu.SMEM)
    out = jax.ShapeDtypeStruct((panel_rows, cols), jnp.float32)
    outs = pl.pallas_call(
        kernel,
        in_specs=[smem] + [vmem] * 6,
        out_specs=[vmem] * 8,
        out_shape=[out] * 8,
        name="regroup",
    )(place, *low, *high)
    return outs[:4], outs[4:]


def chain(place, shares, links, node_count):
    panel_rows = shares[0][0][0].shape[0]
    counts = [low[0].shape[1] for low, _ in shares]
    half = sum(counts) // node_count
    width = 2 * half
    quarter = width // 4
    spots = [
        (run, slice(i * half, (i + 1) * half))
        for run, cols in enumerate(counts)
        for i in range(cols // half)
    ]
    given = 6 * len(shares)

    def kernel(place, *refs):
        links, panels = refs[given : given + 2]
        spread = refs[given + 2 : given + 6]
        columns = refs[given + 6]
        previous = None
        for node, (run, cut) in enumerate(spots):
            low = refs[6 * run : 6 * run + 3]
            high = refs[6 * run + 3 : 6 * run + 6]
            column = -jnp.concatenate(
                [
                    low[0][:, cut] + low[1][:, cut] + low[2][:, cut],
                    high[0][:, cut] + high[1][:, cut] + high[2][:, cut],
                ],
                axis=1,
            )
            if node > 0:
                column = column - times_exact(previous, links[node - 1])
            panels[node] = column.astype(jnp.bfloat16)
            columns[node] = column
            previous = column
        for d in range(4):
            start = pl.multiple_of(lax.rem(place[2] + d, 4) * quarter, quarter)
            spread[d][...] = columns[:, :, pl.ds(start, quarter)]

    vmem = pl.BlockSpec(memory_space=pltpu.VMEM)
    smem = pl.BlockSpec(memory_space=pltpu.SMEM)
    part = jax.ShapeDtypeStruct((node_count, panel_rows, quarter), jnp.float32)
    flat = [array for low, high in shares for array in tuple(low) + tuple(high)]
    outs = pl.pallas_call(
        kernel,
        in_specs=[smem] + [vmem] * (given + 1),
        out_specs=[vmem] * 5,
        out_shape=[jax.ShapeDtypeStruct((node_count, panel_rows, width), jnp.bfloat16)] + [part] * 4,
        scratch_shapes=[pltpu.VMEM((node_count, panel_rows, width), jnp.float32)],
        name="chain",
    )(place, *flat, links)
    return outs[0], outs[1:]


def contraction(place, tiles, block_panels, near, near_other):
    node_count, panel_rows, quarter = block_panels[0].shape
    _, _, piece_rows, width = near.shape
    half = width // 2
    granule = panel_rows // 3
    per_tile = piece_rows * 8 // CAP // granule
    per_piece = piece_rows // granule
    count = 2 * node_count - 1
    strip = half // 32

    def kernel(place, tiles, *refs):
        block_panels = refs[:4]
        near, near_other, keep, send, sums = refs[4:]
        x = place[2]
        k = place[3]
        block = place[0] * 4 + place[1]
        parts = []
        for node in range(node_count):
            first = tiles[node, block * CAP] - block * TPC
            second = tiles[node, block * CAP + 1] - block * TPC
            rows = []
            for d in range(4):
                part = lax.rem(x - d + 4, 4)
                for i in range(3):
                    at = 3 * (2 * part + k) + i
                    tile = at // per_tile
                    inner = at - tile * per_tile
                    in_second = second == tile
                    live = jnp.logical_or(first == tile, in_second)
                    piece = jnp.where(in_second, 8 // CAP, 0) + inner // per_piece
                    start = pl.multiple_of(lax.rem(inner, per_piece) * granule, granule)
                    along = lax.rem(piece // 2 - x + 4, 4)
                    value = jnp.where(
                        lax.rem(piece, 2) == k,
                        near[along, node, pl.ds(start, granule), :],
                        near_other[along, node, pl.ds(start, granule), :],
                    )
                    rows.append(jnp.where(live, value, jnp.zeros_like(value)))
            dense = jnp.concatenate(rows, axis=0)
            parts.append(three_parts(jnp.concatenate([p[node] for p in block_panels], axis=0)))
            right = parts[node] if node == 0 else parts[node] + parts[node - 1]
            out = lax.dot_general(
                dense,
                jnp.concatenate(right, axis=1),
                (((0,), (0,)), ((), ())),
                preferred_element_type=jnp.float32,
            )
            cols = [out[:, i * quarter : (i + 1) * quarter] for i in range(len(right))]
            sums[node] = cols[0] + cols[1] + cols[2]
            if node > 0:
                sums[node_count + node - 1] = cols[3] + cols[4] + cols[5]
        mine = pl.multiple_of(k * half, half)
        theirs = pl.multiple_of((1 - k) * half, half)
        for i in range(count):
            stay = sums[i, pl.ds(mine, half), :].reshape(8, 4, strip, quarter)
            leave = sums[i, pl.ds(theirs, half), :].reshape(8, 4, strip, quarter)
            for y in range(4):
                keep[y, :, i] = stay[:, y]
                send[y, :, i] = leave[:, y]

    out = jax.ShapeDtypeStruct((4, 8, count, strip, quarter), jnp.float32)
    vmem = pl.BlockSpec(memory_space=pltpu.VMEM)
    smem = pl.BlockSpec(memory_space=pltpu.SMEM)
    return pl.pallas_call(
        kernel,
        in_specs=[smem, smem] + [vmem] * 6,
        out_specs=[vmem, vmem],
        out_shape=[out, out],
        scratch_shapes=[pltpu.VMEM((count, width, quarter), jnp.float32)],
        name="contraction",
    )(place, tiles, *block_panels, near, near_other)


def tail(place, plane, other, links, diag_inverse):
    _, _, count, strip, quarter = plane.shape
    node_count, width, _ = diag_inverse.shape

    def kernel(place, plane, other, links, diag_inverse, diagonals, parents, sums):
        k = place[3]
        for source, side in ((plane, k), (other, 1 - k)):
            for y in range(4):
                for x in range(4):
                    for i in range(count):
                        sums[i, side, :, y, :, x * quarter : (x + 1) * quarter] = source[
                            y * 4 + x, :, i
                        ]
        total = [sums[i].reshape(width, width) for i in range(count)]
        diagonal = diag_inverse[0] - total[0]
        diagonals[0] = diagonal
        for node in range(1, node_count):
            link = links[node - 1]
            upper = -(total[node_count + node - 1].T + times_exact(diagonal, link))
            parents[node - 1] = upper
            diagonal = diag_inverse[node] - total[node] - transposed_times(link, upper)
            diagonals[node] = diagonal

    vmem = pl.BlockSpec(memory_space=pltpu.VMEM)
    smem = pl.BlockSpec(memory_space=pltpu.SMEM)
    return pl.pallas_call(
        kernel,
        in_specs=[smem, vmem, vmem, vmem, vmem],
        out_specs=[vmem, vmem],
        out_shape=[
            jax.ShapeDtypeStruct((node_count, width, width), jnp.float32),
            jax.ShapeDtypeStruct((node_count - 1, width, width), jnp.float32),
        ],
        scratch_shapes=[pltpu.VMEM((count, 2, 8, 4, strip, width), jnp.float32)],
        name="tail",
    )(place, plane, other, links, diag_inverse)


def ring_sum(own, behind, middle, ahead, step):
    far_low = step(middle[0], -1)
    far_high = step(middle[1], 1)
    raw_low = step(ahead[0], 1)
    raw_high = step(behind[1], -1)
    low = (own[0], raw_low, step(behind[0] + far_low, -1))
    high = (own[1], raw_high, step(ahead[1] + far_high, 1))
    return low, high


def on_device(ancestor_inverse, factor_slots, slot_tiles, parent_factor, diag_inverse):
    z = lax.axis_index("z")
    y = lax.axis_index("y")
    x = lax.axis_index("x")
    k = lax.axis_index("k")
    place = jnp.stack([z, y, x, k]).astype(jnp.int32)
    block_rows, block_cols = ancestor_inverse.shape
    node_count, piece_rows, width = factor_slots.shape
    panel_rows = block_rows // 32

    split_rows = ancestor_inverse.reshape(4, 4, 2, panel_rows, block_cols)
    leaving = picked(split_rows, 1 - k, 2)
    first_piece, leaving = lax.optimization_barrier((to_column(factor_slots), leaving))
    handed = swap_cores(leaving)

    behind = []
    ahead = []
    moving_up = moving_down = first_piece
    for i in range(4):
        if i == 1:
            mine = after(factor_slots, moving_up)
            near = [mine] + [step_x(mine, -d) for d in range(1, 4)]
        if i == 2:
            moving_up, moving_down, *near = lax.optimization_barrier((moving_up, moving_down, *near))
            near = stacked(near)
            near_other = swap_cores(near)
        if i == 3:
            moving_up, near_other = lax.optimization_barrier((moving_up, near_other))
        moving_up = step_z(moving_up, 1)
        behind.append(moving_up)
        if i < 3:
            moving_down = step_z(moving_down, -1)
            ahead.append(moving_down)
    own_pieces = behind[::-1] + [first_piece] + ahead

    other_groups = [
        (batch, swap_cores(stacked([own_pieces[i] for i in batch])))
        for batch in ((2, 3, 4, 5, 6), (0, 1, 7))
    ]
    middle = products(place, slot_tiles, split_rows, handed, own_pieces, other_groups, (2,), 0)
    rest = products(
        after(place, middle[0]), slot_tiles, split_rows, handed, own_pieces, other_groups, (3, 1, 0), 0
    )
    low, high = ring_sum(rest[4:6], rest[0:2], middle, rest[2:4], step_first)
    low, high = regroup(place, low, high)
    low, high = ring_sum(
        (low[0], high[0]), (low[3], high[3]), (low[2], high[2]), (low[1], high[1]), step_second
    )
    panels, spread = chain(place, [(low, high)], parent_factor, node_count)

    block_panels = [spread[0]] + [step_x(spread[d], d) for d in range(1, 4)]
    keep, send = contraction(place, slot_tiles, block_panels, near, near_other)
    sums = jnp.sum(lax.all_to_all(keep + swap_cores(send), "y", 0, 0, tiled=True), axis=0)
    sums = jnp.sum(lax.all_to_all(sums, "z", 0, 0, tiled=True), axis=0)
    over_z = lax.all_to_all(jnp.broadcast_to(sums, (8,) + sums.shape), "z", 0, 0, tiled=True)
    plane = lax.all_to_all(
        jnp.broadcast_to(over_z, (16,) + over_z.shape), ("y", "x"), 0, 0, tiled=True
    )
    diagonals, parents = tail(place, plane, swap_cores(plane), parent_factor, diag_inverse)
    return panels, diagonals, parents


def solution(mesh):
    grid = Mesh(mesh.devices.reshape(SIZES), AXES)
    placed = (P("z", ("y", "x", "k")), P(None, AXES, None), P(), P(), P())
    return jax.shard_map(
        on_device,
        mesh=grid,
        in_specs=placed,
        out_specs=(P(None, AXES, None), P(), P()),
        check_vma=False,
    )
```

```python
import jax
import jax.numpy as jnp
from jax import lax
from jax.experimental import pallas as pl
from jax.experimental.pallas import tpu as pltpu
from jax.sharding import Mesh, PartitionSpec as P

AXES = ("z", "y", "x", "k")
SIZES = (8, 4, 4, 2)
CAP = 2
TPC = 3


def number(z, y, x, k):
    return ((z % 8 * 4 + y % 4) * 4 + x % 4) * 2 + k % 2


def hop(value, move):
    pairs = []
    for z in range(8):
        for y in range(4):
            for x in range(4):
                for k in range(2):
                    pairs.append((number(z, y, x, k), number(*move(z, y, x, k))))
    return lax.ppermute(value, AXES, pairs)


def swap_cores(value):
    return hop(value, lambda z, y, x, k: (z, y, x, k + 1))


def step_x(value, by):
    return hop(value, lambda z, y, x, k: (z, y, x + by, k))


def step_first(value, by):
    return hop(value, lambda z, y, x, k: (z, y + by * k, x + by * (1 - k), k))


def step_second(value, by):
    return hop(value, lambda z, y, x, k: (z, y + by * (1 - k), x + by * k, k))


def step_z(value, by):
    return hop(value, lambda z, y, x, k: (z + by, y, x, k))


def to_column(value):
    count = 256
    pairs = [(b * 8 + j, j * 32 + b) for b in range(count // 8) for j in range(8)]
    return lax.ppermute(value, AXES, pairs)


def after(value, other):
    return lax.optimization_barrier((value, other))[0]


def picked(value, index, axis):
    return lax.dynamic_index_in_dim(value, index, axis, keepdims=False)


def three_parts(value):
    high = value.astype(jnp.bfloat16)
    rest = value - high.astype(jnp.float32)
    middle = rest.astype(jnp.bfloat16)
    low = (rest - middle.astype(jnp.float32)).astype(jnp.bfloat16)
    return high, middle, low


def times_exact(value, matrix):
    rows = value.shape[0]
    out = jnp.dot(
        jnp.concatenate(three_parts(value), axis=0), matrix, preferred_element_type=jnp.float32
    )
    return out[:rows] + out[rows : 2 * rows] + out[2 * rows :]


def transposed_times(matrix, value):
    cols = value.shape[1]
    out = lax.dot_general(
        matrix,
        jnp.concatenate(three_parts(value), axis=1),
        (((0,), (0,)), ((), ())),
        preferred_element_type=jnp.float32,
    )
    return out[:, :cols] + out[:, cols : 2 * cols] + out[:, 2 * cols :]


def stacked(pieces):
    count = len(pieces)

    def kernel(*refs):
        for i in range(count):
            refs[count][i] = refs[i][...]

    return pl.pallas_call(
        kernel,
        out_shape=jax.ShapeDtypeStruct((count,) + pieces[0].shape, pieces[0].dtype),
        name="stacked" + str(count),
    )(*pieces)


def products(place, tiles, split_rows, handed, own_pieces, other_pieces, offsets, base):
    _, _, _, panel_rows, block_cols = split_rows.shape
    node_count, piece_rows, width = own_pieces[0].shape
    tile_rows = block_cols // TPC
    half = width // 2
    per_slot = tile_rows // piece_rows
    spans = len(offsets)

    def offset_of(i):
        where = jnp.int32(offsets[0])
        for at in range(1, spans):
            where = jnp.where(i == at, offsets[at], where)
        return where

    def kernel(place, tiles, *refs):
        columns = (refs[0:4], refs[4:8])
        pieces = (refs[8:16], refs[16:24])
        outs = refs[24:-3]
        slots, left, sums = refs[-3:]
        node = pl.program_id(1)
        z = place[0]
        first = (place[1] * 4 + place[2]) * 2
        for side, block in ((0, first + place[3]), (1, first + 1 - place[3])):
            names = [tiles[base + node, block * CAP + member] for member in range(CAP)]
            for i in range(8):
                at = lax.rem(z + i + 4, 8)
                live = jnp.where(at < per_slot, names[0], names[1]) >= 0
                rows = pieces[side][i][0]
                slots[side * 8 + at] = jnp.where(live, rows, jnp.zeros_like(rows))
            for member in range(CAP):
                tile = jnp.clip(names[member] - block * TPC, 0, TPC - 1)
                at = pl.ds(pl.multiple_of(tile * tile_rows, tile_rows), tile_rows)
                to = (side * CAP + member) * tile_rows
                for j in range(4):
                    left[j * panel_rows : (j + 1) * panel_rows, to : to + tile_rows] = columns[side][
                        j
                    ][..., at].reshape(panel_rows, tile_rows)

        def column_group(i, carry):
            right = slots[:, :, pl.ds(pl.multiple_of(i * half, half), half)]
            sums[i] = jnp.dot(
                left[...],
                right.reshape(2 * CAP * tile_rows, half),
                preferred_element_type=jnp.float32,
            )
            return carry

        lax.fori_loop(0, 2, column_group, 0)
        for at in range(spans):

            @pl.when(pl.program_id(0) == at)
            def _():
                outs[2 * at][...] = sums[0].reshape(4, panel_rows, half)
                outs[2 * at + 1][...] = sums[1].reshape(4, panel_rows, half)

    def at_chip(j, d, p):
        along_y = jnp.where(p[3] == 0, j, lax.rem(p[1] + offset_of(d), 4))
        along_x = jnp.where(p[3] == 0, lax.rem(p[2] + offset_of(d), 4), j)
        return along_y, along_x

    def kept_at(j):
        return lambda d, i, p, t: at_chip(j, d, p) + (p[3], 0, 0)

    def given_at(j):
        return lambda d, i, p, t: at_chip(j, d, p) + (0, 0)

    def out_at(at):
        return lambda d, i, p, t: (
            0,
            0,
            jnp.where(d == at, i, jnp.where(d < at, 0, node_count - 1)),
        )

    strip = (panel_rows, block_cols)
    out = jax.ShapeDtypeStruct((4, panel_rows, node_count * half), jnp.float32)
    return pl.pallas_call(
        kernel,
        grid_spec=pltpu.PrefetchScalarGridSpec(
            num_scalar_prefetch=2,
            grid=(spans, node_count),
            in_specs=[pl.BlockSpec((1, 1, 1) + strip, kept_at(j)) for j in range(4)]
            + [pl.BlockSpec((1, 1) + strip, given_at(j)) for j in range(4)]
            + [pl.BlockSpec((1, piece_rows, width), lambda d, i, p, t: (i, 0, 0))] * 16,
            out_specs=[
                pl.BlockSpec((4, panel_rows, half), out_at(at)) for at in range(spans) for _ in range(2)
            ],
            scratch_shapes=[
                pltpu.VMEM((16, piece_rows, width), jnp.bfloat16),
                pltpu.VMEM((4 * panel_rows, 2 * CAP * tile_rows), jnp.bfloat16),
                pltpu.VMEM((2, 4 * panel_rows, half), jnp.float32),
            ],
        ),
        out_shape=[out] * (2 * spans),
        name="products" + str(base) + str(spans),
    )(place, tiles, *[split_rows] * 4, *[handed] * 4, *own_pieces, *other_pieces)


def regroup(place, low, high):
    _, panel_rows, cols = low[0].shape

    def kernel(place, *refs):
        here = jnp.where(place[3] == 0, place[1], place[2])
        for group in range(2):
            first, second, third = refs[3 * group : 3 * group + 3]
            for e in range(4):
                at = lax.rem(here + e, 4)
                refs[6 + 4 * group + e][...] = first[at] + second[at] + third[at]

    vmem = pl.BlockSpec(memory_space=pltpu.VMEM)
    smem = pl.BlockSpec(memory_space=pltpu.SMEM)
    out = jax.ShapeDtypeStruct((panel_rows, cols), jnp.float32)
    outs = pl.pallas_call(
        kernel,
        in_specs=[smem] + [vmem] * 6,
        out_specs=[vmem] * 8,
        out_shape=[out] * 8,
        name="regroup",
    )(place, *low, *high)
    return outs[:4], outs[4:]


def chain(place, shares, links, node_count):
    panel_rows = shares[0][0][0].shape[0]
    counts = [low[0].shape[1] for low, _ in shares]
    half = sum(counts) // node_count
    width = 2 * half
    quarter = width // 4
    spots = [
        (run, slice(i * half, (i + 1) * half))
        for run, cols in enumerate(counts)
        for i in range(cols // half)
    ]
    given = 6 * len(shares)

    def kernel(place, *refs):
        links, panels = refs[given : given + 2]
        spread = refs[given + 2 : given + 6]
        columns = refs[given + 6]
        previous = None
        for node, (run, cut) in enumerate(spots):
            low = refs[6 * run : 6 * run + 3]
            high = refs[6 * run + 3 : 6 * run + 6]
            column = -jnp.concatenate(
                [
                    low[0][:, cut] + low[1][:, cut] + low[2][:, cut],
                    high[0][:, cut] + high[1][:, cut] + high[2][:, cut],
                ],
                axis=1,
            )
            if node > 0:
                column = column - times_exact(previous, links[node - 1])
            panels[node] = column.astype(jnp.bfloat16)
            columns[node] = column
            previous = column
        for d in range(4):
            start = pl.multiple_of(lax.rem(place[2] + d, 4) * quarter, quarter)
            spread[d][...] = columns[:, :, pl.ds(start, quarter)]

    vmem = pl.BlockSpec(memory_space=pltpu.VMEM)
    smem = pl.BlockSpec(memory_space=pltpu.SMEM)
    part = jax.ShapeDtypeStruct((node_count, panel_rows, quarter), jnp.float32)
    flat = [array for low, high in shares for array in tuple(low) + tuple(high)]
    outs = pl.pallas_call(
        kernel,
        in_specs=[smem] + [vmem] * (given + 1),
        out_specs=[vmem] * 5,
        out_shape=[jax.ShapeDtypeStruct((node_count, panel_rows, width), jnp.bfloat16)] + [part] * 4,
        scratch_shapes=[pltpu.VMEM((node_count, panel_rows, width), jnp.float32)],
        name="chain",
    )(place, *flat, links)
    return outs[0], outs[1:]


def contraction(place, tiles, block_panels, near):
    node_count, panel_rows, quarter = block_panels[0].shape
    _, _, piece_rows, width = near.shape
    half = width // 2
    granule = panel_rows // 3
    per_tile = piece_rows * 8 // CAP // granule
    per_piece = piece_rows // granule
    count = 2 * node_count - 1
    strip = half // 32

    def kernel(place, tiles, *refs):
        block_panels = refs[:4]
        near, keep, send, sums = refs[4:]
        x = place[2]
        k = place[3]
        block = place[0] * 4 + place[1]
        parts = []
        for node in range(node_count):
            first = tiles[node, block * CAP] - block * TPC
            second = tiles[node, block * CAP + 1] - block * TPC
            rows = []
            for d in range(4):
                part = lax.rem(x - d + 4, 4)
                for i in range(3):
                    at = 3 * (2 * part + k) + i
                    tile = at // per_tile
                    inner = at - tile * per_tile
                    in_second = second == tile
                    live = jnp.logical_or(first == tile, in_second)
                    piece = jnp.where(in_second, 8 // CAP, 0) + inner // per_piece
                    start = pl.multiple_of(lax.rem(inner, per_piece) * granule, granule)
                    side = jnp.where(lax.rem(piece, 2) == k, 0, 4)
                    along = lax.rem(piece // 2 - x + 4, 4)
                    value = near[side + along, node, pl.ds(start, granule), :]
                    rows.append(jnp.where(live, value, jnp.zeros_like(value)))
            dense = jnp.concatenate(rows, axis=0)
            parts.append(three_parts(jnp.concatenate([p[node] for p in block_panels], axis=0)))
            right = parts[node] if node == 0 else parts[node] + parts[node - 1]
            out = lax.dot_general(
                dense,
                jnp.concatenate(right, axis=1),
                (((0,), (0,)), ((), ())),
                preferred_element_type=jnp.float32,
            )
            cols = [out[:, i * quarter : (i + 1) * quarter] for i in range(len(right))]
            sums[node] = cols[0] + cols[1] + cols[2]
            if node > 0:
                sums[node_count + node - 1] = cols[3] + cols[4] + cols[5]
        mine = pl.multiple_of(k * half, half)
        theirs = pl.multiple_of((1 - k) * half, half)
        for i in range(count):
            stay = sums[i, pl.ds(mine, half), :].reshape(8, 4, strip, quarter)
            leave = sums[i, pl.ds(theirs, half), :].reshape(8, 4, strip, quarter)
            for y in range(4):
                keep[y, :, i] = stay[:, y]
                send[y, :, i] = leave[:, y]

    out = jax.ShapeDtypeStruct((4, 8, count, strip, quarter), jnp.float32)
    vmem = pl.BlockSpec(memory_space=pltpu.VMEM)
    smem = pl.BlockSpec(memory_space=pltpu.SMEM)
    return pl.pallas_call(
        kernel,
        in_specs=[smem, smem] + [vmem] * 5,
        out_specs=[vmem, vmem],
        out_shape=[out, out],
        scratch_shapes=[pltpu.VMEM((count, width, quarter), jnp.float32)],
        name="contraction",
    )(place, tiles, *block_panels, near)


def tail(place, plane, other, links, diag_inverse):
    _, _, count, strip, quarter = plane.shape
    node_count, width, _ = diag_inverse.shape

    def kernel(place, plane, other, links, diag_inverse, diagonals, parents, sums):
        k = place[3]

        def place_sum(i, carry):
            for source, side in ((plane, k), (other, 1 - k)):
                for y in range(4):
                    for x in range(4):
                        sums[i, side, :, y, :, x * quarter : (x + 1) * quarter] = source[
                            y * 4 + x, :, i
                        ]
            return carry

        lax.fori_loop(0, count, place_sum, 0)
        total = [sums[i].reshape(width, width) for i in range(count)]
        diagonal = diag_inverse[0] - total[0]
        diagonals[0] = diagonal
        for node in range(1, node_count):
            link = links[node - 1]
            upper = -(total[node_count + node - 1].T + times_exact(diagonal, link))
            parents[node - 1] = upper
            diagonal = diag_inverse[node] - total[node] - transposed_times(link, upper)
            diagonals[node] = diagonal

    vmem = pl.BlockSpec(memory_space=pltpu.VMEM)
    smem = pl.BlockSpec(memory_space=pltpu.SMEM)
    return pl.pallas_call(
        kernel,
        in_specs=[smem, vmem, vmem, vmem, vmem],
        out_specs=[vmem, vmem],
        out_shape=[
            jax.ShapeDtypeStruct((node_count, width, width), jnp.float32),
            jax.ShapeDtypeStruct((node_count - 1, width, width), jnp.float32),
        ],
        scratch_shapes=[pltpu.VMEM((count, 2, 8, 4, strip, width), jnp.float32)],
        name="tail",
    )(place, plane, other, links, diag_inverse)


def ring_sum(own, behind, middle, ahead, step):
    far_low = step(middle[0], -1)
    far_high = step(middle[1], 1)
    raw_low = step(ahead[0], 1)
    raw_high = step(behind[1], -1)
    low = (own[0], raw_low, step(behind[0] + far_low, -1))
    high = (own[1], raw_high, step(ahead[1] + far_high, 1))
    return low, high


def on_device(ancestor_inverse, factor_slots, slot_tiles, parent_factor, diag_inverse):
    z = lax.axis_index("z")
    y = lax.axis_index("y")
    x = lax.axis_index("x")
    k = lax.axis_index("k")
    place = jnp.stack([z, y, x, k]).astype(jnp.int32)
    block_rows, block_cols = ancestor_inverse.shape
    node_count, piece_rows, width = factor_slots.shape
    panel_rows = block_rows // 32

    split_rows = ancestor_inverse.reshape(4, 4, 2, panel_rows, block_cols)
    leaving = picked(split_rows, 1 - k, 2)
    next_x = step_x(factor_slots, -1)
    last_x = step_x(factor_slots, 1)
    first_piece, leaving, next_x, last_x = lax.optimization_barrier(
        (to_column(factor_slots), leaving, next_x, last_x)
    )
    handed = swap_cores(leaving)
    far_x = hop(
        jnp.where(k == 0, next_x, last_x), lambda z, y, x, k: (z, y, x + 2 * k - 1, k)
    )
    near = [factor_slots, next_x, far_x, last_x]

    behind = []
    ahead = []
    other_behind = []
    other_ahead = []
    moving_up = moving_down = first_piece
    other_first = swap_cores(first_piece)
    for i in range(4):
        if i == 2:
            moving_up, other_first = lax.optimization_barrier((moving_up, other_first))
        if i == 3:
            moving_up, other_behind[0], other_ahead[0], *near = lax.optimization_barrier(
                (moving_up, other_behind[0], other_ahead[0], *near)
            )
        moving_up = step_z(moving_up, 1)
        behind.append(moving_up)
        other_behind.append(swap_cores(moving_up))
        if i < 3:
            moving_down = step_z(moving_down, -1)
            ahead.append(moving_down)
            other_ahead.append(swap_cores(moving_down))
    own_pieces = behind[::-1] + [first_piece] + ahead
    other_pieces = other_behind[::-1] + [other_first] + other_ahead

    middle = products(place, slot_tiles, split_rows, handed, own_pieces, other_pieces, (2,), 0)
    rest = products(
        after(place, middle[0]), slot_tiles, split_rows, handed, own_pieces, other_pieces, (3, 1, 0), 0
    )
    near[0] = after(near[0], rest[0])
    near = stacked(near + [swap_cores(piece) for piece in near])
    low, high = ring_sum(rest[4:6], rest[0:2], middle, rest[2:4], step_first)
    place, near = lax.optimization_barrier((place, near))
    low, high = regroup(place, low, high)
    low, high = ring_sum(
        (low[0], high[0]), (low[3], high[3]), (low[2], high[2]), (low[1], high[1]), step_second
    )
    panels, spread = chain(place, [(low, high)], parent_factor, node_count)

    block_panels = [spread[0]] + [step_x(spread[d], d) for d in range(1, 4)]
    keep, send = contraction(place, slot_tiles, block_panels, near)
    sums = jnp.sum(lax.all_to_all(keep + swap_cores(send), "y", 0, 0, tiled=True), axis=0)
    sums = jnp.sum(lax.all_to_all(sums, "z", 0, 0, tiled=True), axis=0)
    over_z = lax.all_to_all(jnp.broadcast_to(sums, (8,) + sums.shape), "z", 0, 0, tiled=True)
    plane = lax.all_to_all(
        jnp.broadcast_to(over_z, (16,) + over_z.shape), ("y", "x"), 0, 0, tiled=True
    )
    diagonals, parents = tail(place, plane, swap_cores(plane), parent_factor, diag_inverse)
    return panels, diagonals, parents


def solution(mesh):
    grid = Mesh(mesh.devices.reshape(SIZES), AXES)
    placed = (P("z", ("y", "x", "k")), P(None, AXES, None), P(), P(), P())
    return jax.shard_map(
        on_device,
        mesh=grid,
        in_specs=placed,
        out_specs=(P(None, AXES, None), P(), P()),
        check_vma=False,
    )
```

```python
import jax
import jax.numpy as jnp
from jax import lax
from jax.experimental import pallas as pl
from jax.experimental.pallas import tpu as pltpu
from jax.sharding import Mesh, PartitionSpec as P

AXES = ("z", "y", "x", "k")
SIZES = (8, 4, 4, 2)
CAP = 2
TPC = 3


def number(z, y, x, k):
    return ((z % 8 * 4 + y % 4) * 4 + x % 4) * 2 + k % 2


def hop(value, move):
    pairs = []
    for z in range(8):
        for y in range(4):
            for x in range(4):
                for k in range(2):
                    pairs.append((number(z, y, x, k), number(*move(z, y, x, k))))
    return lax.ppermute(value, AXES, pairs)


def swap_cores(value):
    return hop(value, lambda z, y, x, k: (z, y, x, k + 1))


def step_x(value, by):
    return hop(value, lambda z, y, x, k: (z, y, x + by, k))


def step_first(value, by):
    return hop(value, lambda z, y, x, k: (z, y + by * k, x + by * (1 - k), k))


def step_second(value, by):
    return hop(value, lambda z, y, x, k: (z, y + by * (1 - k), x + by * k, k))


def step_z(value, by):
    return hop(value, lambda z, y, x, k: (z + by, y, x, k))


def to_column(value):
    count = 256
    pairs = [(b * 8 + j, j * 32 + b) for b in range(count // 8) for j in range(8)]
    return lax.ppermute(value, AXES, pairs)


def after(value, other):
    return lax.optimization_barrier((value, other))[0]


def picked(value, index, axis):
    return lax.dynamic_index_in_dim(value, index, axis, keepdims=False)


def three_parts(value):
    high = value.astype(jnp.bfloat16)
    rest = value - high.astype(jnp.float32)
    middle = rest.astype(jnp.bfloat16)
    low = (rest - middle.astype(jnp.float32)).astype(jnp.bfloat16)
    return high, middle, low


def times_exact(value, matrix):
    rows = value.shape[0]
    out = jnp.dot(
        jnp.concatenate(three_parts(value), axis=0), matrix, preferred_element_type=jnp.float32
    )
    return out[:rows] + out[rows : 2 * rows] + out[2 * rows :]


def transposed_times(matrix, value):
    cols = value.shape[1]
    out = lax.dot_general(
        matrix,
        jnp.concatenate(three_parts(value), axis=1),
        (((0,), (0,)), ((), ())),
        preferred_element_type=jnp.float32,
    )
    return out[:, :cols] + out[:, cols : 2 * cols] + out[:, 2 * cols :]


def stacked(pieces):
    count = len(pieces)

    def kernel(*refs):
        for i in range(count):
            refs[count][i] = refs[i][...]

    return pl.pallas_call(
        kernel,
        out_shape=jax.ShapeDtypeStruct((count,) + pieces[0].shape, pieces[0].dtype),
        name="stacked" + str(count),
    )(*pieces)


def products(place, tiles, split_rows, handed, own_pieces, other_pieces, offsets, base):
    _, _, _, panel_rows, block_cols = split_rows.shape
    node_count, piece_rows, width = own_pieces[0].shape
    tile_rows = block_cols // TPC
    half = width // 2
    per_slot = tile_rows // piece_rows
    spans = len(offsets)

    def offset_of(i):
        where = jnp.int32(offsets[0])
        for at in range(1, spans):
            where = jnp.where(i == at, offsets[at], where)
        return where

    def kernel(place, tiles, *refs):
        columns = (refs[0:4], refs[4:8])
        pieces = (refs[8:16], refs[16:24])
        outs = refs[24:-1]
        slots = refs[-1]
        node = pl.program_id(1)
        z = place[0]
        first = (place[1] * 4 + place[2]) * 2
        sums = [None, None]
        for side, block in ((0, first + place[3]), (1, first + 1 - place[3])):
            for i in range(8):
                piece = pieces[side][i][...].reshape(piece_rows, width)
                slots[side, lax.rem(z + i + 4, 8)] = piece
            for member in range(CAP):
                name = tiles[base + node, block * CAP + member]
                tile = jnp.clip(name - block * TPC, 0, TPC - 1)
                at = pl.ds(pl.multiple_of(tile * tile_rows, tile_rows), tile_rows)
                rows = slots[side, member * per_slot : (member + 1) * per_slot]
                rows = rows.reshape(tile_rows, width)
                rows = jnp.where(name >= 0, rows, jnp.zeros_like(rows))
                left = jnp.concatenate(
                    [part[..., at].reshape(panel_rows, tile_rows) for part in columns[side]], axis=0
                )
                for i in range(2):
                    term = jnp.dot(
                        left, rows[:, i * half : (i + 1) * half], preferred_element_type=jnp.float32
                    )
                    sums[i] = term if sums[i] is None else sums[i] + term
        for at in range(spans):

            @pl.when(pl.program_id(0) == at)
            def _():
                outs[2 * at][...] = sums[0].reshape(4, panel_rows, half)
                outs[2 * at + 1][...] = sums[1].reshape(4, panel_rows, half)

    def at_chip(j, d, p):
        along_y = jnp.where(p[3] == 0, j, lax.rem(p[1] + offset_of(d), 4))
        along_x = jnp.where(p[3] == 0, lax.rem(p[2] + offset_of(d), 4), j)
        return along_y, along_x

    def kept_at(j):
        return lambda d, i, p, t: at_chip(j, d, p) + (p[3], 0, 0)

    def given_at(j):
        return lambda d, i, p, t: at_chip(j, d, p) + (0, 0)

    def out_at(at):
        return lambda d, i, p, t: (
            0,
            0,
            jnp.where(d == at, i, jnp.where(d < at, 0, node_count - 1)),
        )

    def other_at(at):
        return pl.BlockSpec((1, 1, piece_rows, width), lambda d, i, p, t: (at, i, 0, 0))

    strip = (panel_rows, block_cols)
    out = jax.ShapeDtypeStruct((4, panel_rows, node_count * half), jnp.float32)
    return pl.pallas_call(
        kernel,
        grid_spec=pltpu.PrefetchScalarGridSpec(
            num_scalar_prefetch=2,
            grid=(spans, node_count),
            in_specs=[pl.BlockSpec((1, 1, 1) + strip, kept_at(j)) for j in range(4)]
            + [pl.BlockSpec((1, 1) + strip, given_at(j)) for j in range(4)]
            + [pl.BlockSpec((1, piece_rows, width), lambda d, i, p, t: (i, 0, 0))] * 8
            + [other_at(at) for _, at in other_pieces],
            out_specs=[
                pl.BlockSpec((4, panel_rows, half), out_at(at)) for at in range(spans) for _ in range(2)
            ],
            scratch_shapes=[pltpu.VMEM((2, 8, piece_rows, width), jnp.bfloat16)],
        ),
        out_shape=[out] * (2 * spans),
        name="products" + str(offsets[0]),
    )(place, tiles, *[split_rows] * 4, *[handed] * 4, *own_pieces, *[array for array, _ in other_pieces])


def regroup(place, low, high, offsets):
    _, panel_rows, cols = low[0].shape
    count = len(offsets)

    def at_offset(at):
        def index(i, p):
            here = jnp.where(p[3] == 0, p[1], p[2])
            return lax.rem(here + offsets[at], 4), 0, 0

        return pl.BlockSpec((1, panel_rows, cols), index)

    def kernel(place, *refs):
        for at in range(2 * count):
            first, second, third = refs[3 * at : 3 * at + 3]
            refs[6 * count + at][...] = first[0] + second[0] + third[0]

    out = jax.ShapeDtypeStruct((panel_rows, cols), jnp.float32)
    outs = pl.pallas_call(
        kernel,
        grid_spec=pltpu.PrefetchScalarGridSpec(
            num_scalar_prefetch=1,
            grid=(1,),
            in_specs=[at_offset(at) for at in range(count) for _ in range(6)],
            out_specs=[pl.BlockSpec((panel_rows, cols), lambda i, p: (0, 0))] * (2 * count),
        ),
        out_shape=[out] * (2 * count),
        name="regroup" + str(count),
    )(place, *(list(low) + list(high)) * count)
    return [(outs[2 * at], outs[2 * at + 1]) for at in range(count)]


def chain(place, shares, links, node_count):
    panel_rows = shares[0][0][0].shape[0]
    counts = [low[0].shape[1] for low, _ in shares]
    half = sum(counts) // node_count
    width = 2 * half
    quarter = width // 4
    spots = [
        (run, slice(i * half, (i + 1) * half))
        for run, cols in enumerate(counts)
        for i in range(cols // half)
    ]
    given = 6 * len(shares)

    def kernel(place, *refs):
        links, panels = refs[given : given + 2]
        spread = refs[given + 2 : given + 6]
        columns = refs[given + 6]
        previous = None
        for node, (run, cut) in enumerate(spots):
            low = refs[6 * run : 6 * run + 3]
            high = refs[6 * run + 3 : 6 * run + 6]
            column = -jnp.concatenate(
                [
                    low[0][:, cut] + low[1][:, cut] + low[2][:, cut],
                    high[0][:, cut] + high[1][:, cut] + high[2][:, cut],
                ],
                axis=1,
            )
            if node > 0:
                column = column - times_exact(previous, links[node - 1])
            panels[node] = column.astype(jnp.bfloat16)
            columns[node] = column
            previous = column
        for d in range(4):
            start = pl.multiple_of(lax.rem(place[2] + d, 4) * quarter, quarter)
            spread[d][...] = columns[:, :, pl.ds(start, quarter)]

    vmem = pl.BlockSpec(memory_space=pltpu.VMEM)
    smem = pl.BlockSpec(memory_space=pltpu.SMEM)
    part = jax.ShapeDtypeStruct((node_count, panel_rows, quarter), jnp.float32)
    flat = [array for low, high in shares for array in tuple(low) + tuple(high)]
    outs = pl.pallas_call(
        kernel,
        in_specs=[smem] + [vmem] * (given + 1),
        out_specs=[vmem] * 5,
        out_shape=[jax.ShapeDtypeStruct((node_count, panel_rows, width), jnp.bfloat16)] + [part] * 4,
        scratch_shapes=[pltpu.VMEM((node_count, panel_rows, width), jnp.float32)],
        name="chain",
    )(place, *flat, links)
    return outs[0], outs[1:]


def contraction(place, tiles, block_panels, near, near_other):
    node_count, panel_rows, quarter = block_panels[0].shape
    _, _, piece_rows, width = near.shape
    half = width // 2
    granule = panel_rows // 3
    per_tile = piece_rows * 8 // CAP // granule
    per_piece = piece_rows // granule
    count = 2 * node_count - 1
    strip = half // 32

    def kernel(place, tiles, *refs):
        block_panels = refs[:4]
        near, near_other, keep, send, sums = refs[4:]
        x = place[2]
        k = place[3]
        block = place[0] * 4 + place[1]
        parts = []
        for node in range(node_count):
            first = tiles[node, block * CAP] - block * TPC
            second = tiles[node, block * CAP + 1] - block * TPC
            rows = []
            for d in range(4):
                part = lax.rem(x - d + 4, 4)
                for i in range(3):
                    at = 3 * (2 * part + k) + i
                    tile = at // per_tile
                    inner = at - tile * per_tile
                    in_second = second == tile
                    live = jnp.logical_or(first == tile, in_second)
                    piece = jnp.where(in_second, 8 // CAP, 0) + inner // per_piece
                    start = pl.multiple_of(lax.rem(inner, per_piece) * granule, granule)
                    along = lax.rem(piece // 2 - x + 4, 4)
                    value = jnp.where(
                        lax.rem(piece, 2) == k,
                        near[along, node, pl.ds(start, granule), :],
                        near_other[along, node, pl.ds(start, granule), :],
                    )
                    rows.append(jnp.where(live, value, jnp.zeros_like(value)))
            dense = jnp.concatenate(rows, axis=0)
            parts.append(three_parts(jnp.concatenate([p[node] for p in block_panels], axis=0)))
            right = parts[node] if node == 0 else parts[node] + parts[node - 1]
            out = lax.dot_general(
                dense,
                jnp.concatenate(right, axis=1),
                (((0,), (0,)), ((), ())),
                preferred_element_type=jnp.float32,
            )
            cols = [out[:, i * quarter : (i + 1) * quarter] for i in range(len(right))]
            sums[node] = cols[0] + cols[1] + cols[2]
            if node > 0:
                sums[node_count + node - 1] = cols[3] + cols[4] + cols[5]
        mine = pl.multiple_of(k * half, half)
        theirs = pl.multiple_of((1 - k) * half, half)
        for i in range(count):
            stay = sums[i, pl.ds(mine, half), :].reshape(8, 4, strip, quarter)
            leave = sums[i, pl.ds(theirs, half), :].reshape(8, 4, strip, quarter)
            for y in range(4):
                keep[y, :, i] = stay[:, y]
                send[y, :, i] = leave[:, y]

    out = jax.ShapeDtypeStruct((4, 8, count, strip, quarter), jnp.float32)
    vmem = pl.BlockSpec(memory_space=pltpu.VMEM)
    smem = pl.BlockSpec(memory_space=pltpu.SMEM)
    return pl.pallas_call(
        kernel,
        in_specs=[smem, smem] + [vmem] * 6,
        out_specs=[vmem, vmem],
        out_shape=[out, out],
        scratch_shapes=[pltpu.VMEM((count, width, quarter), jnp.float32)],
        name="contraction",
    )(place, tiles, *block_panels, near, near_other)


def tail(place, plane, other, links, diag_inverse):
    _, _, count, strip, quarter = plane.shape
    node_count, width, _ = diag_inverse.shape

    def kernel(place, plane, other, links, diag_inverse, diagonals, parents, sums):
        k = place[3]

        def place_sum(i, carry):
            for source, side in ((plane, k), (other, 1 - k)):
                for y in range(4):
                    for x in range(4):
                        sums[i, side, :, y, :, x * quarter : (x + 1) * quarter] = source[
                            y * 4 + x, :, i
                        ]
            return carry

        lax.fori_loop(0, count, place_sum, 0)
        total = [sums[i].reshape(width, width) for i in range(count)]
        diagonal = diag_inverse[0] - total[0]
        diagonals[0] = diagonal
        for node in range(1, node_count):
            link = links[node - 1]
            upper = -(total[node_count + node - 1].T + times_exact(diagonal, link))
            parents[node - 1] = upper
            diagonal = diag_inverse[node] - total[node] - transposed_times(link, upper)
            diagonals[node] = diagonal

    vmem = pl.BlockSpec(memory_space=pltpu.VMEM)
    smem = pl.BlockSpec(memory_space=pltpu.SMEM)
    return pl.pallas_call(
        kernel,
        in_specs=[smem, vmem, vmem, vmem, vmem],
        out_specs=[vmem, vmem],
        out_shape=[
            jax.ShapeDtypeStruct((node_count, width, width), jnp.float32),
            jax.ShapeDtypeStruct((node_count - 1, width, width), jnp.float32),
        ],
        scratch_shapes=[pltpu.VMEM((count, 2, 8, 4, strip, width), jnp.float32)],
        name="tail",
    )(place, plane, other, links, diag_inverse)


def ring_sum(own, behind, middle, ahead, step):
    far_low = step(middle[0], -1)
    far_high = step(middle[1], 1)
    raw_low = step(ahead[0], 1)
    raw_high = step(behind[1], -1)
    low = (own[0], raw_low, step(behind[0] + far_low, -1))
    high = (own[1], raw_high, step(ahead[1] + far_high, 1))
    return low, high


def on_device(ancestor_inverse, factor_slots, slot_tiles, parent_factor, diag_inverse):
    z = lax.axis_index("z")
    y = lax.axis_index("y")
    x = lax.axis_index("x")
    k = lax.axis_index("k")
    place = jnp.stack([z, y, x, k]).astype(jnp.int32)
    block_rows, block_cols = ancestor_inverse.shape
    node_count, piece_rows, width = factor_slots.shape
    panel_rows = block_rows // 32

    split_rows = ancestor_inverse.reshape(4, 4, 2, panel_rows, block_cols)
    leaving = picked(split_rows, 1 - k, 2)
    next_x = step_x(factor_slots, -1)
    last_x = step_x(factor_slots, 1)
    first_piece, leaving, next_x, last_x = lax.optimization_barrier(
        (to_column(factor_slots), leaving, next_x, last_x)
    )
    handed = swap_cores(leaving)
    far_x = hop(
        jnp.where(k == 0, next_x, last_x), lambda z, y, x, k: (z, y, x + 2 * k - 1, k)
    )
    near = [factor_slots, next_x, far_x, last_x]

    behind = []
    ahead = []
    moving_up = moving_down = first_piece
    for i in range(4):
        if i == 2:
            early = swap_cores(stacked([behind[0], first_piece, ahead[0]]))
        if i == 3:
            later = swap_cores(stacked([behind[1], ahead[1]]))
            moving_up, early, *near = lax.optimization_barrier((moving_up, early, *near))
        moving_up = step_z(moving_up, 1)
        behind.append(moving_up)
        if i < 3:
            moving_down = step_z(moving_down, -1)
            ahead.append(moving_down)
    own_pieces = behind[::-1] + [first_piece] + ahead
    other_pieces = [(swap_cores(piece)[None], 0) for piece in (behind[3], behind[2])]
    other_pieces += [(later, 0), (early, 0), (early, 1), (early, 2), (later, 1)]
    other_pieces += [(swap_cores(ahead[2])[None], 0)]

    def shares(offsets, place):
        return products(
            place, slot_tiles, split_rows, handed, own_pieces, other_pieces, offsets, 0
        )

    middle = shares((2,), place)
    raw = shares((3, 1), after(place, middle[0]))
    own = shares((0,), after(place, raw[0]))
    near[0] = after(near[0], own[0])
    near = stacked(near)
    near_other = swap_cores(near)
    low, high = ring_sum(own, raw[0:2], middle, raw[2:4], step_first)
    place, near, near_other = lax.optimization_barrier((place, near, near_other))
    (far,) = regroup(place, low, high, (2,))
    ahead_share, behind_share, own_share = regroup(after(place, far[0]), low, high, (1, 3, 0))
    low, high = ring_sum(own_share, behind_share, far, ahead_share, step_second)
    panels, spread = chain(place, [(low, high)], parent_factor, node_count)

    block_panels = [spread[0]] + [step_x(spread[d], d) for d in range(1, 4)]
    keep, send = contraction(place, slot_tiles, block_panels, near, near_other)
    sums = jnp.sum(lax.all_to_all(keep + swap_cores(send), "y", 0, 0, tiled=True), axis=0)
    sums = jnp.sum(lax.all_to_all(sums, "z", 0, 0, tiled=True), axis=0)
    over_z = lax.all_to_all(jnp.broadcast_to(sums, (8,) + sums.shape), "z", 0, 0, tiled=True)
    plane = lax.all_to_all(
        jnp.broadcast_to(over_z, (16,) + over_z.shape), ("y", "x"), 0, 0, tiled=True
    )
    diagonals, parents = tail(place, plane, swap_cores(plane), parent_factor, diag_inverse)
    return panels, diagonals, parents


def solution(mesh):
    grid = Mesh(mesh.devices.reshape(SIZES), AXES)
    placed = (P("z", ("y", "x", "k")), P(None, AXES, None), P(), P(), P())
    return jax.shard_map(
        on_device,
        mesh=grid,
        in_specs=placed,
        out_specs=(P(None, AXES, None), P(), P()),
        check_vma=False,
    )
```

```python
import jax
import jax.numpy as jnp
from jax import lax
from jax.experimental import pallas as pl
from jax.experimental.pallas import tpu as pltpu
from jax.sharding import Mesh, PartitionSpec as P

AXES = ("z", "y", "x", "k")
SIZES = (8, 4, 4, 2)
CAP = 2
TPC = 3


def number(z, y, x, k):
    return ((z % 8 * 4 + y % 4) * 4 + x % 4) * 2 + k % 2


def hop(value, move):
    pairs = []
    for z in range(8):
        for y in range(4):
            for x in range(4):
                for k in range(2):
                    pairs.append((number(z, y, x, k), number(*move(z, y, x, k))))
    return lax.ppermute(value, AXES, pairs)


def swap_cores(value):
    return hop(value, lambda z, y, x, k: (z, y, x, k + 1))


def step_x(value, by):
    return hop(value, lambda z, y, x, k: (z, y, x + by, k))


def step_first(value, by):
    return hop(value, lambda z, y, x, k: (z, y + by * k, x + by * (1 - k), k))


def step_second(value, by):
    return hop(value, lambda z, y, x, k: (z, y + by * (1 - k), x + by * k, k))


def step_z(value, by):
    return hop(value, lambda z, y, x, k: (z + by, y, x, k))


def to_column(value):
    count = 256
    pairs = [(b * 8 + j, j * 32 + b) for b in range(count // 8) for j in range(8)]
    return lax.ppermute(value, AXES, pairs)


def after(value, other):
    return lax.optimization_barrier((value, other))[0]


def picked(value, index, axis):
    return lax.dynamic_index_in_dim(value, index, axis, keepdims=False)


def two_parts(value):
    high = value.astype(jnp.bfloat16)
    return high, (value - high.astype(jnp.float32)).astype(jnp.bfloat16)


def times_split(value, matrix):
    rows = value.shape[0]
    out = jnp.dot(
        jnp.concatenate(two_parts(value), axis=0), matrix, preferred_element_type=jnp.float32
    )
    return out[:rows] + out[rows:]


def transposed_times(matrix, value):
    cols = value.shape[1]
    out = lax.dot_general(
        matrix,
        jnp.concatenate(two_parts(value), axis=1),
        (((0,), (0,)), ((), ())),
        preferred_element_type=jnp.float32,
    )
    return out[:, :cols] + out[:, cols:]


def stacked(pieces):
    count = len(pieces)

    def kernel(*refs):
        for i in range(count):
            refs[count][i] = refs[i][...]

    return pl.pallas_call(
        kernel,
        out_shape=jax.ShapeDtypeStruct((count,) + pieces[0].shape, pieces[0].dtype),
        name="stacked" + str(count),
    )(*pieces)


def products(place, tiles, split_rows, handed, own_pieces, other_pieces, offsets, base):
    _, _, _, panel_rows, block_cols = split_rows.shape
    node_count, piece_rows, width = own_pieces[0].shape
    tile_rows = block_cols // TPC
    half = width // 2
    per_slot = tile_rows // piece_rows
    spans = len(offsets)

    def offset_of(i):
        where = jnp.int32(offsets[0])
        for at in range(1, spans):
            where = jnp.where(i == at, offsets[at], where)
        return where

    def kernel(place, tiles, *refs):
        columns = (refs[0:4], refs[4:8])
        pieces = (refs[8:16], refs[16:24])
        outs = refs[24:-1]
        slots = refs[-1]
        node = pl.program_id(1)
        z = place[0]
        first = (place[1] * 4 + place[2]) * 2
        sums = [None, None]
        for side, block in ((0, first + place[3]), (1, first + 1 - place[3])):
            for i in range(8):
                piece = pieces[side][i][...].reshape(piece_rows, width)
                slots[side, lax.rem(z + i + 4, 8)] = piece
            for member in range(CAP):
                name = tiles[base + node, block * CAP + member]
                tile = jnp.clip(name - block * TPC, 0, TPC - 1)
                at = pl.ds(pl.multiple_of(tile * tile_rows, tile_rows), tile_rows)
                rows = slots[side, member * per_slot : (member + 1) * per_slot]
                rows = rows.reshape(tile_rows, width)
                rows = jnp.where(name >= 0, rows, jnp.zeros_like(rows))
                left = jnp.concatenate(
                    [part[..., at].reshape(panel_rows, tile_rows) for part in columns[side]], axis=0
                )
                for i in range(2):
                    term = jnp.dot(
                        left, rows[:, i * half : (i + 1) * half], preferred_element_type=jnp.float32
                    )
                    sums[i] = term if sums[i] is None else sums[i] + term
        for at in range(spans):

            @pl.when(pl.program_id(0) == at)
            def _():
                outs[2 * at][...] = sums[0].reshape(4, panel_rows, half)
                outs[2 * at + 1][...] = sums[1].reshape(4, panel_rows, half)

    def at_chip(j, d, p):
        along_y = jnp.where(p[3] == 0, j, lax.rem(p[1] + offset_of(d), 4))
        along_x = jnp.where(p[3] == 0, lax.rem(p[2] + offset_of(d), 4), j)
        return along_y, along_x

    def kept_at(j):
        return lambda d, i, p, t: at_chip(j, d, p) + (p[3], 0, 0)

    def given_at(j):
        return lambda d, i, p, t: at_chip(j, d, p) + (0, 0)

    def out_at(at):
        return lambda d, i, p, t: (
            0,
            0,
            jnp.where(d == at, i, jnp.where(d < at, 0, node_count - 1)),
        )

    strip = (panel_rows, block_cols)
    out = jax.ShapeDtypeStruct((4, panel_rows, node_count * half), jnp.float32)
    return pl.pallas_call(
        kernel,
        grid_spec=pltpu.PrefetchScalarGridSpec(
            num_scalar_prefetch=2,
            grid=(spans, node_count),
            in_specs=[pl.BlockSpec((1, 1, 1) + strip, kept_at(j)) for j in range(4)]
            + [pl.BlockSpec((1, 1) + strip, given_at(j)) for j in range(4)]
            + [pl.BlockSpec((1, piece_rows, width), lambda d, i, p, t: (i, 0, 0))] * 16,
            out_specs=[
                pl.BlockSpec((4, panel_rows, half), out_at(at)) for at in range(spans) for _ in range(2)
            ],
            scratch_shapes=[pltpu.VMEM((2, 8, piece_rows, width), jnp.bfloat16)],
        ),
        out_shape=[out] * (2 * spans),
        name="products" + str(offsets[0]),
    )(place, tiles, *[split_rows] * 4, *[handed] * 4, *own_pieces, *other_pieces)


def regroup(place, low, high, offsets):
    _, panel_rows, cols = low[0].shape
    count = len(offsets)

    def at_offset(at):
        def index(i, p):
            here = jnp.where(p[3] == 0, p[1], p[2])
            return lax.rem(here + offsets[at], 4), 0, 0

        return pl.BlockSpec((1, panel_rows, cols), index)

    def kernel(place, *refs):
        for at in range(2 * count):
            first, second, third = refs[3 * at : 3 * at + 3]
            refs[6 * count + at][...] = first[0] + second[0] + third[0]

    out = jax.ShapeDtypeStruct((panel_rows, cols), jnp.float32)
    outs = pl.pallas_call(
        kernel,
        grid_spec=pltpu.PrefetchScalarGridSpec(
            num_scalar_prefetch=1,
            grid=(1,),
            in_specs=[at_offset(at) for at in range(count) for _ in range(6)],
            out_specs=[pl.BlockSpec((panel_rows, cols), lambda i, p: (0, 0))] * (2 * count),
        ),
        out_shape=[out] * (2 * count),
        name="regroup" + str(offsets[0]),
    )(place, *(list(low) + list(high)) * count)
    return [(outs[2 * at], outs[2 * at + 1]) for at in range(count)]


def chain(place, shares, links, node_count):
    panel_rows = shares[0][0][0].shape[0]
    counts = [low[0].shape[1] for low, _ in shares]
    half = sum(counts) // node_count
    width = 2 * half
    quarter = width // 4
    spots = [
        (run, slice(i * half, (i + 1) * half))
        for run, cols in enumerate(counts)
        for i in range(cols // half)
    ]
    given = 6 * len(shares)

    def kernel(place, *refs):
        links, panels = refs[given : given + 2]
        spread = refs[given + 2 : given + 6]
        columns = refs[given + 6]
        previous = None
        for node, (run, cut) in enumerate(spots):
            low = refs[6 * run : 6 * run + 3]
            high = refs[6 * run + 3 : 6 * run + 6]
            column = -jnp.concatenate(
                [
                    low[0][:, cut] + low[1][:, cut] + low[2][:, cut],
                    high[0][:, cut] + high[1][:, cut] + high[2][:, cut],
                ],
                axis=1,
            )
            if node > 0:
                column = column - times_split(previous, links[node - 1])
            panels[node] = column.astype(jnp.bfloat16)
            columns[node] = column
            previous = column
        for d in range(4):
            start = pl.multiple_of(lax.rem(place[2] + d, 4) * quarter, quarter)
            spread[d][...] = columns[:, :, pl.ds(start, quarter)]

    vmem = pl.BlockSpec(memory_space=pltpu.VMEM)
    smem = pl.BlockSpec(memory_space=pltpu.SMEM)
    part = jax.ShapeDtypeStruct((node_count, panel_rows, quarter), jnp.float32)
    flat = [array for low, high in shares for array in tuple(low) + tuple(high)]
    outs = pl.pallas_call(
        kernel,
        in_specs=[smem] + [vmem] * (given + 1),
        out_specs=[vmem] * 5,
        out_shape=[jax.ShapeDtypeStruct((node_count, panel_rows, width), jnp.bfloat16)] + [part] * 4,
        scratch_shapes=[pltpu.VMEM((node_count, panel_rows, width), jnp.float32)],
        name="chain",
    )(place, *flat, links)
    return outs[0], outs[1:]


def contraction(place, tiles, block_panels, near, near_other):
    node_count, panel_rows, quarter = block_panels[0].shape
    _, _, piece_rows, width = near.shape
    half = width // 2
    granule = panel_rows // 3
    per_tile = piece_rows * 8 // CAP // granule
    per_piece = piece_rows // granule
    count = 2 * node_count - 1
    strip = half // 32

    def kernel(place, tiles, *refs):
        block_panels = refs[:4]
        near, near_other, keep, send, sums = refs[4:]
        x = place[2]
        k = place[3]
        block = place[0] * 4 + place[1]
        parts = []
        for node in range(node_count):
            first = tiles[node, block * CAP] - block * TPC
            second = tiles[node, block * CAP + 1] - block * TPC
            rows = []
            for d in range(4):
                part = lax.rem(x - d + 4, 4)
                for i in range(3):
                    at = 3 * (2 * part + k) + i
                    tile = at // per_tile
                    inner = at - tile * per_tile
                    in_second = second == tile
                    live = jnp.logical_or(first == tile, in_second)
                    piece = jnp.where(in_second, 8 // CAP, 0) + inner // per_piece
                    start = pl.multiple_of(lax.rem(inner, per_piece) * granule, granule)
                    along = lax.rem(piece // 2 - x + 4, 4)
                    value = jnp.where(
                        lax.rem(piece, 2) == k,
                        near[along, node, pl.ds(start, granule), :],
                        near_other[along, node, pl.ds(start, granule), :],
                    )
                    rows.append(jnp.where(live, value, jnp.zeros_like(value)))
            dense = jnp.concatenate(rows, axis=0)
            parts.append(two_parts(jnp.concatenate([p[node] for p in block_panels], axis=0)))
            right = parts[node] if node == 0 else parts[node] + parts[node - 1]
            out = lax.dot_general(
                dense,
                jnp.concatenate(right, axis=1),
                (((0,), (0,)), ((), ())),
                preferred_element_type=jnp.float32,
            )
            cols = [out[:, i * quarter : (i + 1) * quarter] for i in range(len(right))]
            sums[node] = cols[0] + cols[1]
            if node > 0:
                sums[node_count + node - 1] = cols[2] + cols[3]
        mine = pl.multiple_of(k * half, half)
        theirs = pl.multiple_of((1 - k) * half, half)
        for i in range(count):
            stay = sums[i, pl.ds(mine, half), :].reshape(8, 4, strip, quarter)
            leave = sums[i, pl.ds(theirs, half), :].reshape(8, 4, strip, quarter)
            for y in range(4):
                keep[y, :, i] = stay[:, y]
                send[y, :, i] = leave[:, y]

    out = jax.ShapeDtypeStruct((4, 8, count, strip, quarter), jnp.float32)
    vmem = pl.BlockSpec(memory_space=pltpu.VMEM)
    smem = pl.BlockSpec(memory_space=pltpu.SMEM)
    return pl.pallas_call(
        kernel,
        in_specs=[smem, smem] + [vmem] * 6,
        out_specs=[vmem, vmem],
        out_shape=[out, out],
        scratch_shapes=[pltpu.VMEM((count, width, quarter), jnp.float32)],
        name="contraction",
    )(place, tiles, *block_panels, near, near_other)


def tail(place, plane, other, links, diag_inverse):
    _, _, count, strip, quarter = plane.shape
    node_count, width, _ = diag_inverse.shape

    def kernel(place, plane, other, links, diag_inverse, diagonals, parents, sums):
        k = place[3]

        def place_sum(i, carry):
            for source, side in ((plane, k), (other, 1 - k)):
                for y in range(4):
                    for x in range(4):
                        sums[i, side, :, y, :, x * quarter : (x + 1) * quarter] = source[
                            y * 4 + x, :, i
                        ]
            return carry

        lax.fori_loop(0, count, place_sum, 0)
        diagonals[0] = diag_inverse[0] - sums[0].reshape(width, width)

        def finish(node, carry):
            link = links[node - 1]
            second = sums[node_count + node - 1].reshape(width, width).T
            upper = -(second + times_split(diagonals[node - 1], link))
            parents[node - 1] = upper
            first = sums[node].reshape(width, width)
            diagonals[node] = diag_inverse[node] - first - transposed_times(link, upper)
            return carry

        lax.fori_loop(1, node_count, finish, 0)

    vmem = pl.BlockSpec(memory_space=pltpu.VMEM)
    smem = pl.BlockSpec(memory_space=pltpu.SMEM)
    return pl.pallas_call(
        kernel,
        in_specs=[smem, vmem, vmem, vmem, vmem],
        out_specs=[vmem, vmem],
        out_shape=[
            jax.ShapeDtypeStruct((node_count, width, width), jnp.float32),
            jax.ShapeDtypeStruct((node_count - 1, width, width), jnp.float32),
        ],
        scratch_shapes=[pltpu.VMEM((count, 2, 8, 4, strip, width), jnp.float32)],
        name="tail",
    )(place, plane, other, links, diag_inverse)


def ring_sum(own, behind, middle, ahead, step):
    far_low = step(middle[0], -1)
    far_high = step(middle[1], 1)
    raw_low = step(ahead[0], 1)
    raw_high = step(behind[1], -1)
    low = (own[0], raw_low, step(behind[0] + far_low, -1))
    high = (own[1], raw_high, step(ahead[1] + far_high, 1))
    return low, high


def on_device(ancestor_inverse, factor_slots, slot_tiles, parent_factor, diag_inverse):
    z = lax.axis_index("z")
    y = lax.axis_index("y")
    x = lax.axis_index("x")
    k = lax.axis_index("k")
    place = jnp.stack([z, y, x, k]).astype(jnp.int32)
    block_rows, block_cols = ancestor_inverse.shape
    node_count, piece_rows, width = factor_slots.shape
    panel_rows = block_rows // 32

    split_rows = ancestor_inverse.reshape(4, 4, 2, panel_rows, block_cols)
    leaving = picked(split_rows, 1 - k, 2)
    next_x = step_x(factor_slots, -1)
    last_x = step_x(factor_slots, 1)
    first_piece, leaving, next_x, last_x = lax.optimization_barrier(
        (to_column(factor_slots), leaving, next_x, last_x)
    )
    handed = swap_cores(leaving)
    far_x = hop(
        jnp.where(k == 0, next_x, last_x), lambda z, y, x, k: (z, y, x + 2 * k - 1, k)
    )
    near = [factor_slots, next_x, far_x, last_x]

    behind = []
    ahead = []
    other_behind = []
    other_ahead = []
    moving_up = moving_down = first_piece
    other_first = swap_cores(first_piece)
    for i in range(4):
        if i == 2:
            moving_up, other_first = lax.optimization_barrier((moving_up, other_first))
        if i == 3:
            moving_up, other_behind[0], other_ahead[0], handed, *near = lax.optimization_barrier(
                (moving_up, other_behind[0], other_ahead[0], handed, *near)
            )
        moving_up = step_z(moving_up, 1)
        behind.append(moving_up)
        other_behind.append(swap_cores(moving_up))
        if i < 3:
            moving_down = step_z(moving_down, -1)
            ahead.append(moving_down)
            other_ahead.append(swap_cores(moving_down))
    own_pieces = behind[::-1] + [first_piece] + ahead
    other_pieces = other_behind[::-1] + [other_first] + other_ahead

    def shares(offsets, place):
        return products(
            place, slot_tiles, split_rows, handed, own_pieces, other_pieces, offsets, 0
        )

    middle = shares((2,), place)
    raw = shares((3, 1), after(place, middle[0]))
    own = shares((0,), after(place, raw[0]))
    near[0] = after(near[0], own[0])
    near = stacked(near)
    near_other = swap_cores(near)
    low, high = ring_sum(own, raw[0:2], middle, raw[2:4], step_first)
    place, near, near_other = lax.optimization_barrier((place, near, near_other))
    (far,) = regroup(place, low, high, (2,))
    ahead_share, behind_share = regroup(after(place, far[0]), low, high, (1, 3))
    (own_share,) = regroup(after(place, ahead_share[0]), low, high, (0,))
    low, high = ring_sum(own_share, behind_share, far, ahead_share, step_second)
    panels, spread = chain(place, [(low, high)], parent_factor, node_count)

    block_panels = [spread[0]] + [step_x(spread[d], d) for d in range(1, 4)]
    keep, send = contraction(place, slot_tiles, block_panels, near, near_other)
    sums = jnp.sum(lax.all_to_all(keep + swap_cores(send), "y", 0, 0, tiled=True), axis=0)
    sums = jnp.sum(lax.all_to_all(sums, "z", 0, 0, tiled=True), axis=0)
    over_z = lax.all_to_all(jnp.broadcast_to(sums, (8,) + sums.shape), "z", 0, 0, tiled=True)
    plane = lax.all_to_all(
        jnp.broadcast_to(over_z, (16,) + over_z.shape), ("y", "x"), 0, 0, tiled=True
    )
    diagonals, parents = tail(place, plane, swap_cores(plane), parent_factor, diag_inverse)
    return panels, diagonals, parents


def solution(mesh):
    grid = Mesh(mesh.devices.reshape(SIZES), AXES)
    placed = (P("z", ("y", "x", "k")), P(None, AXES, None), P(), P(), P())
    return jax.shard_map(
        on_device,
        mesh=grid,
        in_specs=placed,
        out_specs=(P(None, AXES, None), P(), P()),
        check_vma=False,
    )
```

```python
import jax
import jax.numpy as jnp
from jax import lax
from jax.experimental import pallas as pl
from jax.experimental.pallas import tpu as pltpu
from jax.sharding import Mesh, PartitionSpec as P


AXES = ("z", "y", "x", "k")
SIZES = (8, 4, 4, 2)
CAP = 2
TPC = 3


def number(z, y, x, k):
    return ((z % 8 * 4 + y % 4) * 4 + x % 4) * 2 + k % 2


def hop(value, move):
    pairs = []
    for z in range(8):
        for y in range(4):
            for x in range(4):
                for k in range(2):
                    pairs.append((number(z, y, x, k), number(*move(z, y, x, k))))
    return lax.ppermute(value, AXES, pairs)


def swap_cores(value):
    return hop(value, lambda z, y, x, k: (z, y, x, k + 1))


def step_x(value, by):
    return hop(value, lambda z, y, x, k: (z, y, x + by, k))


def step_first(value, by):
    return hop(value, lambda z, y, x, k: (z, y + by * k, x + by * (1 - k), k))


def step_second(value, by):
    return hop(value, lambda z, y, x, k: (z, y + by * (1 - k), x + by * k, k))


def step_z(value, by):
    return hop(value, lambda z, y, x, k: (z + by, y, x, k))


def to_column(value):
    count = 256
    pairs = [(b * 8 + j, j * 32 + b) for b in range(count // 8) for j in range(8)]
    return lax.ppermute(value, AXES, pairs)


def after(value, other):
    return lax.optimization_barrier((value, other))[0]


def picked(value, index, axis):
    return lax.dynamic_index_in_dim(value, index, axis, keepdims=False)


def two_parts(value):
    high = value.astype(jnp.bfloat16)
    return high, (value - high.astype(jnp.float32)).astype(jnp.bfloat16)


def times_split(value, matrix):
    rows = value.shape[0]
    out = jnp.dot(
        jnp.concatenate(two_parts(value), axis=0), matrix, preferred_element_type=jnp.float32
    )
    return out[:rows] + out[rows:]


def transposed_times(matrix, value):
    cols = value.shape[1]
    out = lax.dot_general(
        matrix,
        jnp.concatenate(two_parts(value), axis=1),
        (((0,), (0,)), ((), ())),
        preferred_element_type=jnp.float32,
    )
    return out[:, :cols] + out[:, cols:]


def stacked(pieces):
    count = len(pieces)

    def kernel(*refs):
        for i in range(count):
            refs[count][i] = refs[i][...]

    return pl.pallas_call(
        kernel, out_shape=jax.ShapeDtypeStruct((count,) + pieces[0].shape, pieces[0].dtype)
    )(*pieces)


def products(place, tiles, split_rows, handed, own_pieces, other_pieces, offsets, base):
    _, _, _, panel_rows, block_cols = split_rows.shape
    node_count, piece_rows, width = own_pieces[0].shape
    tile_rows = block_cols // TPC
    half = width // 2
    per_slot = tile_rows // piece_rows
    spans = len(offsets)

    def offset_of(i):
        where = jnp.int32(offsets[0])
        for at in range(1, spans):
            where = jnp.where(i == at, offsets[at], where)
        return where

    def kernel(place, tiles, *refs):
        columns = (refs[0:4], refs[4:8])
        pieces = (refs[8:16], refs[16:24])
        outs = refs[24:-1]
        slots = refs[-1]
        node = pl.program_id(1)
        z = place[0]
        first = (place[1] * 4 + place[2]) * 2
        sums = [None, None]
        for side, block in ((0, first + place[3]), (1, first + 1 - place[3])):
            for i in range(8):
                piece = pieces[side][i][...].reshape(piece_rows, width)
                slots[side, lax.rem(z + i + 4, 8)] = piece
            for member in range(CAP):
                name = tiles[base + node, block * CAP + member]
                tile = jnp.clip(name - block * TPC, 0, TPC - 1)
                at = pl.ds(pl.multiple_of(tile * tile_rows, tile_rows), tile_rows)
                rows = slots[side, member * per_slot : (member + 1) * per_slot]
                rows = rows.reshape(tile_rows, width)
                rows = jnp.where(name >= 0, rows, jnp.zeros_like(rows))
                left = jnp.concatenate(
                    [part[..., at].reshape(panel_rows, tile_rows) for part in columns[side]], axis=0
                )
                for i in range(2):
                    term = jnp.dot(
                        left, rows[:, i * half : (i + 1) * half], preferred_element_type=jnp.float32
                    )
                    sums[i] = term if sums[i] is None else sums[i] + term
        for at in range(spans):

            @pl.when(pl.program_id(0) == at)
            def _():
                outs[2 * at][...] = sums[0].reshape(4, panel_rows, half)
                outs[2 * at + 1][...] = sums[1].reshape(4, panel_rows, half)

    def at_chip(j, d, p):
        along_y = jnp.where(p[3] == 0, j, lax.rem(p[1] + offset_of(d), 4))
        along_x = jnp.where(p[3] == 0, lax.rem(p[2] + offset_of(d), 4), j)
        return along_y, along_x

    def kept_at(j):
        return lambda d, i, p, t: at_chip(j, d, p) + (p[3], 0, 0)

    def given_at(j):
        return lambda d, i, p, t: at_chip(j, d, p) + (0, 0)

    def out_at(at):
        return lambda d, i, p, t: (
            0,
            0,
            jnp.where(d == at, i, jnp.where(d < at, 0, node_count - 1)),
        )

    strip = (panel_rows, block_cols)
    out = jax.ShapeDtypeStruct((4, panel_rows, node_count * half), jnp.float32)
    return pl.pallas_call(
        kernel,
        grid_spec=pltpu.PrefetchScalarGridSpec(
            num_scalar_prefetch=2,
            grid=(spans, node_count),
            in_specs=[pl.BlockSpec((1, 1, 1) + strip, kept_at(j)) for j in range(4)]
            + [pl.BlockSpec((1, 1) + strip, given_at(j)) for j in range(4)]
            + [pl.BlockSpec((1, piece_rows, width), lambda d, i, p, t: (i, 0, 0))] * 16,
            out_specs=[
                pl.BlockSpec((4, panel_rows, half), out_at(at)) for at in range(spans) for _ in range(2)
            ],
            scratch_shapes=[pltpu.VMEM((2, 8, piece_rows, width), jnp.bfloat16)],
        ),
        out_shape=[out] * (2 * spans),
    )(place, tiles, *[split_rows] * 4, *[handed] * 4, *own_pieces, *other_pieces)


def chain(place, shares, links, node_count):
    panel_rows = shares[0][0][0].shape[0]
    counts = [low[0].shape[1] for low, _ in shares]
    half = sum(counts) // node_count
    width = 2 * half
    quarter = width // 4
    spots = [
        (run, slice(i * half, (i + 1) * half))
        for run, cols in enumerate(counts)
        for i in range(cols // half)
    ]
    given = 6 * len(shares)

    def kernel(place, *refs):
        links, panels = refs[given : given + 2]
        spread = refs[given + 2 : given + 6]
        columns = refs[given + 6]
        previous = None
        for node, (run, cut) in enumerate(spots):
            low = refs[6 * run : 6 * run + 3]
            high = refs[6 * run + 3 : 6 * run + 6]
            column = -jnp.concatenate(
                [
                    low[0][:, cut] + low[1][:, cut] + low[2][:, cut],
                    high[0][:, cut] + high[1][:, cut] + high[2][:, cut],
                ],
                axis=1,
            )
            if node > 0:
                column = column - times_split(previous, links[node - 1])
            panels[node] = column.astype(jnp.bfloat16)
            columns[node] = column
            previous = column
        for d in range(4):
            start = pl.multiple_of(lax.rem(place[2] + d, 4) * quarter, quarter)
            spread[d][...] = columns[:, :, pl.ds(start, quarter)]

    vmem = pl.BlockSpec(memory_space=pltpu.VMEM)
    smem = pl.BlockSpec(memory_space=pltpu.SMEM)
    part = jax.ShapeDtypeStruct((node_count, panel_rows, quarter), jnp.float32)
    flat = [array for low, high in shares for array in tuple(low) + tuple(high)]
    outs = pl.pallas_call(
        kernel,
        in_specs=[smem] + [vmem] * (given + 1),
        out_specs=[vmem] * 5,
        out_shape=[jax.ShapeDtypeStruct((node_count, panel_rows, width), jnp.bfloat16)] + [part] * 4,
        scratch_shapes=[pltpu.VMEM((node_count, panel_rows, width), jnp.float32)],
        name="chain",
    )(place, *flat, links)
    return outs[0], outs[1:]


def contraction(place, tiles, block_panels, near, near_other):
    node_count, panel_rows, quarter = block_panels[0].shape
    _, _, piece_rows, width = near.shape
    half = width // 2
    granule = panel_rows // 3
    per_tile = piece_rows * 8 // CAP // granule
    per_piece = piece_rows // granule
    count = 2 * node_count - 1
    strip = half // 32

    def kernel(place, tiles, *refs):
        block_panels = refs[:4]
        near, near_other, keep, send, sums = refs[4:]
        x = place[2]
        k = place[3]
        block = place[0] * 4 + place[1]
        parts = []
        for node in range(node_count):
            first = tiles[node, block * CAP] - block * TPC
            second = tiles[node, block * CAP + 1] - block * TPC
            rows = []
            for d in range(4):
                part = lax.rem(x - d + 4, 4)
                for i in range(3):
                    at = 3 * (2 * part + k) + i
                    tile = at // per_tile
                    inner = at - tile * per_tile
                    in_second = second == tile
                    live = jnp.logical_or(first == tile, in_second)
                    piece = jnp.where(in_second, 8 // CAP, 0) + inner // per_piece
                    start = pl.multiple_of(lax.rem(inner, per_piece) * granule, granule)
                    along = lax.rem(piece // 2 - x + 4, 4)
                    value = jnp.where(
                        lax.rem(piece, 2) == k,
                        near[along, node, pl.ds(start, granule), :],
                        near_other[along, node, pl.ds(start, granule), :],
                    )
                    rows.append(jnp.where(live, value, jnp.zeros_like(value)))
            dense = jnp.concatenate(rows, axis=0)
            parts.append(two_parts(jnp.concatenate([p[node] for p in block_panels], axis=0)))
            right = parts[node] if node == 0 else parts[node] + parts[node - 1]
            out = lax.dot_general(
                dense,
                jnp.concatenate(right, axis=1),
                (((0,), (0,)), ((), ())),
                preferred_element_type=jnp.float32,
            )
            cols = [out[:, i * quarter : (i + 1) * quarter] for i in range(len(right))]
            sums[node] = cols[0] + cols[1]
            if node > 0:
                sums[node_count + node - 1] = cols[2] + cols[3]
        mine = pl.multiple_of(k * half, half)
        theirs = pl.multiple_of((1 - k) * half, half)
        for i in range(count):
            stay = sums[i, pl.ds(mine, half), :].reshape(8, 4, strip, quarter)
            leave = sums[i, pl.ds(theirs, half), :].reshape(8, 4, strip, quarter)
            for y in range(4):
                keep[y, :, i] = stay[:, y]
                send[y, :, i] = leave[:, y]

    out = jax.ShapeDtypeStruct((4, 8, count, strip, quarter), jnp.float32)
    vmem = pl.BlockSpec(memory_space=pltpu.VMEM)
    smem = pl.BlockSpec(memory_space=pltpu.SMEM)
    return pl.pallas_call(
        kernel,
        in_specs=[smem, smem] + [vmem] * 6,
        out_specs=[vmem, vmem],
        out_shape=[out, out],
        scratch_shapes=[pltpu.VMEM((count, width, quarter), jnp.float32)],
        name="contraction",
    )(place, tiles, *block_panels, near, near_other)


def tail(place, plane, other, links, diag_inverse):
    _, _, count, strip, quarter = plane.shape
    node_count, width, _ = diag_inverse.shape

    def kernel(place, plane, other, links, diag_inverse, diagonals, parents, sums):
        k = place[3]

        def place_sum(i, carry):
            for source, side in ((plane, k), (other, 1 - k)):
                for y in range(4):
                    for x in range(4):
                        sums[i, side, :, y, :, x * quarter : (x + 1) * quarter] = source[
                            y * 4 + x, :, i
                        ]
            return carry

        lax.fori_loop(0, count, place_sum, 0)
        diagonals[0] = diag_inverse[0] - sums[0].reshape(width, width)

        def finish(node, carry):
            link = links[node - 1]
            second = sums[node_count + node - 1].reshape(width, width).T
            upper = -(second + times_split(diagonals[node - 1], link))
            parents[node - 1] = upper
            first = sums[node].reshape(width, width)
            diagonals[node] = diag_inverse[node] - first - transposed_times(link, upper)
            return carry

        lax.fori_loop(1, node_count, finish, 0)

    vmem = pl.BlockSpec(memory_space=pltpu.VMEM)
    smem = pl.BlockSpec(memory_space=pltpu.SMEM)
    return pl.pallas_call(
        kernel,
        in_specs=[smem, vmem, vmem, vmem, vmem],
        out_specs=[vmem, vmem],
        out_shape=[
            jax.ShapeDtypeStruct((node_count, width, width), jnp.float32),
            jax.ShapeDtypeStruct((node_count - 1, width, width), jnp.float32),
        ],
        scratch_shapes=[pltpu.VMEM((count, 2, 8, 4, strip, width), jnp.float32)],
        name="tail",
    )(place, plane, other, links, diag_inverse)


def ring_sum(own, behind, middle, ahead, step):
    far_low = step(middle[0], -1)
    far_high = step(middle[1], 1)
    raw_low = step(ahead[0], 1)
    raw_high = step(behind[1], -1)
    joined_low = behind[0] + far_low
    joined_high = ahead[1] + far_high
    low = (own[0], raw_low, step(joined_low, -1))
    high = (own[1], raw_high, step(joined_high, 1))
    return low, high


def on_device(ancestor_inverse, factor_slots, slot_tiles, parent_factor, diag_inverse):
    z = lax.axis_index("z")
    y = lax.axis_index("y")
    x = lax.axis_index("x")
    k = lax.axis_index("k")
    place = jnp.stack([z, y, x, k]).astype(jnp.int32)
    block_rows, block_cols = ancestor_inverse.shape
    node_count, _, _ = factor_slots.shape
    panel_rows = block_rows // 32

    split_rows = ancestor_inverse.reshape(4, 4, 2, panel_rows, block_cols)
    leaving = picked(split_rows, 1 - k, 2)
    next_x = step_x(factor_slots, -1)
    last_x = step_x(factor_slots, 1)
    first_piece, leaving, next_x, last_x = lax.optimization_barrier(
        (to_column(factor_slots), leaving, next_x, last_x)
    )
    handed = swap_cores(leaving)
    far_x = hop(
        jnp.where(k == 0, next_x, last_x), lambda z, y, x, k: (z, y, x + 2 * k - 1, k)
    )
    near = [factor_slots, next_x, far_x, last_x]

    behind = []
    ahead = []
    other_behind = []
    other_ahead = []
    moving_up = moving_down = first_piece
    other_first = swap_cores(first_piece)
    for i in range(4):
        if i == 2:
            moving_up, other_first = lax.optimization_barrier((moving_up, other_first))
        if i == 3:
            moving_up, other_behind[0], other_ahead[0], handed, *near = lax.optimization_barrier(
                (moving_up, other_behind[0], other_ahead[0], handed, *near)
            )
        moving_up = step_z(moving_up, 1)
        behind.append(moving_up)
        other_behind.append(swap_cores(moving_up))
        if i < 3:
            moving_down = step_z(moving_down, -1)
            ahead.append(moving_down)
            other_ahead.append(swap_cores(moving_down))
    own_pieces = behind[::-1] + [first_piece] + ahead
    other_pieces = other_behind[::-1] + [other_first] + other_ahead

    def shares(offsets, place):
        return products(
            place, slot_tiles, split_rows, handed, own_pieces, other_pieces, offsets, 0
        )

    middle = shares((2,), place)
    raw = shares((3, 1), after(place, middle[0]))
    own = shares((0,), after(place, raw[0]))
    near[0] = after(near[0], own[0])
    near = stacked(near)
    near_other = swap_cores(near)
    low, high = ring_sum(own, raw[0:2], middle, raw[2:4], step_first)
    here, near, near_other = lax.optimization_barrier((jnp.where(k == 0, y, x), near, near_other))

    def regroup(offset, here):
        at = (here + offset) % 4
        return [sum(picked(share, at, 0) for share in group) for group in (low, high)]

    far = regroup(2, here)
    here, *far = lax.optimization_barrier((here, *far))
    ahead_share, behind_share = regroup(1, here), regroup(3, here)
    here, *raw = lax.optimization_barrier((here, ahead_share[0], behind_share[1]))
    ahead_share[0], behind_share[1] = raw
    own_share = regroup(0, here)
    low, high = ring_sum(own_share, behind_share, far, ahead_share, step_second)
    panels, spread = chain(place, [(low, high)], parent_factor, node_count)

    block_panels = [spread[0]] + [step_x(spread[d], d) for d in range(1, 4)]
    keep, send = contraction(place, slot_tiles, block_panels, near, near_other)
    sums = jnp.sum(lax.all_to_all(keep + swap_cores(send), "y", 0, 0, tiled=True), axis=0)
    sums = jnp.sum(lax.all_to_all(sums, "z", 0, 0, tiled=True), axis=0)
    over_z = lax.all_to_all(jnp.broadcast_to(sums, (8,) + sums.shape), "z", 0, 0, tiled=True)
    plane = lax.all_to_all(
        jnp.broadcast_to(over_z, (16,) + over_z.shape), ("y", "x"), 0, 0, tiled=True
    )
    diagonals, parents = tail(place, plane, swap_cores(plane), parent_factor, diag_inverse)
    return panels, diagonals, parents


def solution(mesh):
    grid = Mesh(mesh.devices.reshape(SIZES), AXES)
    placed = (P("z", ("y", "x", "k")), P(None, AXES, None), P(), P(), P())
    return jax.shard_map(
        on_device,
        mesh=grid,
        in_specs=placed,
        out_specs=(P(None, AXES, None), P(), P()),
        check_vma=False,
    )
```

```python
import jax
import jax.numpy as jnp
from jax import lax
from jax.experimental import pallas as pl
from jax.experimental.pallas import tpu as pltpu
from jax.sharding import Mesh, PartitionSpec as P


AXES = ("z", "y", "x", "k")
SIZES = (8, 4, 4, 2)
CAP = 2
TPC = 3


def number(z, y, x, k):
    return ((z % 8 * 4 + y % 4) * 4 + x % 4) * 2 + k % 2


def hop(value, move):
    pairs = []
    for z in range(8):
        for y in range(4):
            for x in range(4):
                for k in range(2):
                    pairs.append((number(z, y, x, k), number(*move(z, y, x, k))))
    return lax.ppermute(value, AXES, pairs)


def swap_cores(value):
    return hop(value, lambda z, y, x, k: (z, y, x, k + 1))


def step_x(value, by):
    return hop(value, lambda z, y, x, k: (z, y, x + by, k))


def step_first(value, by):
    return hop(value, lambda z, y, x, k: (z, y + by * k, x + by * (1 - k), k))


def step_second(value, by):
    return hop(value, lambda z, y, x, k: (z, y + by * (1 - k), x + by * k, k))


def step_z(value, by):
    return hop(value, lambda z, y, x, k: (z + by, y, x, k))


def to_column(value):
    count = 256
    pairs = [(b * 8 + j, j * 32 + b) for b in range(count // 8) for j in range(8)]
    return lax.ppermute(value, AXES, pairs)


def after(value, other):
    return lax.optimization_barrier((value, other))[0]


def picked(value, index, axis):
    return lax.dynamic_index_in_dim(value, index, axis, keepdims=False)


def two_parts(value):
    high = value.astype(jnp.bfloat16)
    return high, (value - high.astype(jnp.float32)).astype(jnp.bfloat16)


def times_split(value, matrix):
    rows = value.shape[0]
    out = jnp.dot(
        jnp.concatenate(two_parts(value), axis=0), matrix, preferred_element_type=jnp.float32
    )
    return out[:rows] + out[rows:]


def transposed_times(matrix, value):
    cols = value.shape[1]
    out = lax.dot_general(
        matrix,
        jnp.concatenate(two_parts(value), axis=1),
        (((0,), (0,)), ((), ())),
        preferred_element_type=jnp.float32,
    )
    return out[:, :cols] + out[:, cols:]


def stacked(pieces):
    count = len(pieces)

    def kernel(*refs):
        for i in range(count):
            refs[count][i] = refs[i][...]

    return pl.pallas_call(
        kernel, out_shape=jax.ShapeDtypeStruct((count,) + pieces[0].shape, pieces[0].dtype)
    )(*pieces)


def products(place, tiles, split_rows, handed, own_pieces, other_pieces, offsets, base):
    _, _, _, panel_rows, block_cols = split_rows.shape
    node_count, piece_rows, width = own_pieces[0].shape
    tile_rows = block_cols // TPC
    half = width // 2
    per_slot = tile_rows // piece_rows
    spans = len(offsets)

    def offset_of(i):
        where = jnp.int32(offsets[0])
        for at in range(1, spans):
            where = jnp.where(i == at, offsets[at], where)
        return where

    def kernel(place, tiles, *refs):
        columns = (refs[0:4], refs[4:8])
        pieces = (refs[8:16], refs[16:24])
        outs = refs[24:-1]
        slots = refs[-1]
        node = pl.program_id(1)
        z = place[0]
        first = (place[1] * 4 + place[2]) * 2
        sums = [None, None]
        for side, block in ((0, first + place[3]), (1, first + 1 - place[3])):
            for i in range(8):
                piece = pieces[side][i][...].reshape(piece_rows, width)
                slots[side, lax.rem(z + i + 4, 8)] = piece
            for member in range(CAP):
                name = tiles[base + node, block * CAP + member]
                tile = jnp.clip(name - block * TPC, 0, TPC - 1)
                at = pl.ds(pl.multiple_of(tile * tile_rows, tile_rows), tile_rows)
                rows = slots[side, member * per_slot : (member + 1) * per_slot]
                rows = rows.reshape(tile_rows, width)
                rows = jnp.where(name >= 0, rows, jnp.zeros_like(rows))
                left = jnp.concatenate(
                    [part[..., at].reshape(panel_rows, tile_rows) for part in columns[side]], axis=0
                )
                for i in range(2):
                    term = jnp.dot(
                        left, rows[:, i * half : (i + 1) * half], preferred_element_type=jnp.float32
                    )
                    sums[i] = term if sums[i] is None else sums[i] + term
        for at in range(spans):

            @pl.when(pl.program_id(0) == at)
            def _():
                outs[2 * at][...] = sums[0].reshape(4, panel_rows, half)
                outs[2 * at + 1][...] = sums[1].reshape(4, panel_rows, half)

    def at_chip(j, d, p):
        along_y = jnp.where(p[3] == 0, j, lax.rem(p[1] + offset_of(d), 4))
        along_x = jnp.where(p[3] == 0, lax.rem(p[2] + offset_of(d), 4), j)
        return along_y, along_x

    def kept_at(j):
        return lambda d, i, p, t: at_chip(j, d, p) + (p[3], 0, 0)

    def given_at(j):
        return lambda d, i, p, t: at_chip(j, d, p) + (0, 0)

    def out_at(at):
        return lambda d, i, p, t: (
            0,
            0,
            jnp.where(d == at, i, jnp.where(d < at, 0, node_count - 1)),
        )

    strip = (panel_rows, block_cols)
    out = jax.ShapeDtypeStruct((4, panel_rows, node_count * half), jnp.float32)
    return pl.pallas_call(
        kernel,
        grid_spec=pltpu.PrefetchScalarGridSpec(
            num_scalar_prefetch=2,
            grid=(spans, node_count),
            in_specs=[pl.BlockSpec((1, 1, 1) + strip, kept_at(j)) for j in range(4)]
            + [pl.BlockSpec((1, 1) + strip, given_at(j)) for j in range(4)]
            + [pl.BlockSpec((1, piece_rows, width), lambda d, i, p, t: (i, 0, 0))] * 16,
            out_specs=[
                pl.BlockSpec((4, panel_rows, half), out_at(at)) for at in range(spans) for _ in range(2)
            ],
            scratch_shapes=[pltpu.VMEM((2, 8, piece_rows, width), jnp.bfloat16)],
        ),
        out_shape=[out] * (2 * spans),
    )(place, tiles, *[split_rows] * 4, *[handed] * 4, *own_pieces, *other_pieces)


def chain(place, shares, links, node_count):
    panel_rows = shares[0][0][0].shape[0]
    counts = [low[0].shape[1] for low, _ in shares]
    half = sum(counts) // node_count
    width = 2 * half
    quarter = width // 4
    spots = [
        (run, slice(i * half, (i + 1) * half))
        for run, cols in enumerate(counts)
        for i in range(cols // half)
    ]
    given = 6 * len(shares)

    def kernel(place, *refs):
        links, panels = refs[given : given + 2]
        spread = refs[given + 2 : given + 6]
        columns = refs[given + 6]
        previous = None
        for node, (run, cut) in enumerate(spots):
            low = refs[6 * run : 6 * run + 3]
            high = refs[6 * run + 3 : 6 * run + 6]
            column = -jnp.concatenate(
                [
                    low[0][:, cut] + low[1][:, cut] + low[2][:, cut],
                    high[0][:, cut] + high[1][:, cut] + high[2][:, cut],
                ],
                axis=1,
            )
            if node > 0:
                column = column - times_split(previous, links[node - 1])
            panels[node] = column.astype(jnp.bfloat16)
            columns[node] = column
            previous = column
        for d in range(4):
            start = pl.multiple_of(lax.rem(place[2] + d, 4) * quarter, quarter)
            spread[d][...] = columns[:, :, pl.ds(start, quarter)]

    vmem = pl.BlockSpec(memory_space=pltpu.VMEM)
    smem = pl.BlockSpec(memory_space=pltpu.SMEM)
    part = jax.ShapeDtypeStruct((node_count, panel_rows, quarter), jnp.float32)
    flat = [array for low, high in shares for array in tuple(low) + tuple(high)]
    outs = pl.pallas_call(
        kernel,
        in_specs=[smem] + [vmem] * (given + 1),
        out_specs=[vmem] * 5,
        out_shape=[jax.ShapeDtypeStruct((node_count, panel_rows, width), jnp.bfloat16)] + [part] * 4,
        scratch_shapes=[pltpu.VMEM((node_count, panel_rows, width), jnp.float32)],
        name="chain",
    )(place, *flat, links)
    return outs[0], outs[1:]


def contraction(place, tiles, block_panels, near, near_other):
    node_count, panel_rows, quarter = block_panels[0].shape
    _, _, piece_rows, width = near.shape
    half = width // 2
    granule = panel_rows // 3
    per_tile = piece_rows * 8 // CAP // granule
    per_piece = piece_rows // granule
    count = 2 * node_count - 1
    strip = half // 32

    def kernel(place, tiles, *refs):
        block_panels = refs[:4]
        near, near_other, keep, send, sums = refs[4:]
        x = place[2]
        k = place[3]
        block = place[0] * 4 + place[1]
        parts = []
        for node in range(node_count):
            first = tiles[node, block * CAP] - block * TPC
            second = tiles[node, block * CAP + 1] - block * TPC
            rows = []
            for d in range(4):
                part = lax.rem(x - d + 4, 4)
                for i in range(3):
                    at = 3 * (2 * part + k) + i
                    tile = at // per_tile
                    inner = at - tile * per_tile
                    in_second = second == tile
                    live = jnp.logical_or(first == tile, in_second)
                    piece = jnp.where(in_second, 8 // CAP, 0) + inner // per_piece
                    start = pl.multiple_of(lax.rem(inner, per_piece) * granule, granule)
                    along = lax.rem(piece // 2 - x + 4, 4)
                    value = jnp.where(
                        lax.rem(piece, 2) == k,
                        near[along, node, pl.ds(start, granule), :],
                        near_other[along, node, pl.ds(start, granule), :],
                    )
                    rows.append(jnp.where(live, value, jnp.zeros_like(value)))
            dense = jnp.concatenate(rows, axis=0)
            parts.append(two_parts(jnp.concatenate([p[node] for p in block_panels], axis=0)))
            right = parts[node] if node == 0 else parts[node] + parts[node - 1]
            out = lax.dot_general(
                dense,
                jnp.concatenate(right, axis=1),
                (((0,), (0,)), ((), ())),
                preferred_element_type=jnp.float32,
            )
            cols = [out[:, i * quarter : (i + 1) * quarter] for i in range(len(right))]
            sums[node] = cols[0] + cols[1]
            if node > 0:
                sums[node_count + node - 1] = cols[2] + cols[3]
        mine = pl.multiple_of(k * half, half)
        theirs = pl.multiple_of((1 - k) * half, half)
        for i in range(count):
            stay = sums[i, pl.ds(mine, half), :].reshape(8, 4, strip, quarter)
            leave = sums[i, pl.ds(theirs, half), :].reshape(8, 4, strip, quarter)
            for y in range(4):
                keep[y, :, i] = stay[:, y]
                send[y, :, i] = leave[:, y]

    out = jax.ShapeDtypeStruct((4, 8, count, strip, quarter), jnp.float32)
    vmem = pl.BlockSpec(memory_space=pltpu.VMEM)
    smem = pl.BlockSpec(memory_space=pltpu.SMEM)
    return pl.pallas_call(
        kernel,
        in_specs=[smem, smem] + [vmem] * 6,
        out_specs=[vmem, vmem],
        out_shape=[out, out],
        scratch_shapes=[pltpu.VMEM((count, width, quarter), jnp.float32)],
        name="contraction",
    )(place, tiles, *block_panels, near, near_other)


def tail(place, plane, other, links, diag_inverse):
    _, _, count, strip, quarter = plane.shape
    node_count, width, _ = diag_inverse.shape

    def kernel(place, plane, other, links, diag_inverse, diagonals, parents, sums):
        k = place[3]

        def place_sum(i, carry):
            for source, side in ((plane, k), (other, 1 - k)):
                for y in range(4):
                    for x in range(4):
                        sums[i, side, :, y, :, x * quarter : (x + 1) * quarter] = source[
                            y * 4 + x, :, i
                        ]
            return carry

        lax.fori_loop(0, count, place_sum, 0)
        diagonals[0] = diag_inverse[0] - sums[0].reshape(width, width)

        def finish(node, carry):
            link = links[node - 1]
            second = sums[node_count + node - 1].reshape(width, width).T
            upper = -(second + times_split(diagonals[node - 1], link))
            parents[node - 1] = upper
            first = sums[node].reshape(width, width)
            diagonals[node] = diag_inverse[node] - first - transposed_times(link, upper)
            return carry

        lax.fori_loop(1, node_count, finish, 0)

    vmem = pl.BlockSpec(memory_space=pltpu.VMEM)
    smem = pl.BlockSpec(memory_space=pltpu.SMEM)
    return pl.pallas_call(
        kernel,
        in_specs=[smem, vmem, vmem, vmem, vmem],
        out_specs=[vmem, vmem],
        out_shape=[
            jax.ShapeDtypeStruct((node_count, width, width), jnp.float32),
            jax.ShapeDtypeStruct((node_count - 1, width, width), jnp.float32),
        ],
        scratch_shapes=[pltpu.VMEM((count, 2, 8, 4, strip, width), jnp.float32)],
        name="tail",
    )(place, plane, other, links, diag_inverse)


def ring_sum(own, behind, middle, ahead, step):
    far_low = step(middle[0], -1)
    far_high = step(middle[1], 1)
    raw_low = step(ahead[0], 1)
    raw_high = step(behind[1], -1)
    joined_low = behind[0] + far_low
    joined_high = ahead[1] + far_high
    low = (own[0], raw_low, step(joined_low, -1))
    high = (own[1], raw_high, step(joined_high, 1))
    return low, high


def on_device(ancestor_inverse, factor_slots, slot_tiles, parent_factor, diag_inverse):
    z = lax.axis_index("z")
    y = lax.axis_index("y")
    x = lax.axis_index("x")
    k = lax.axis_index("k")
    place = jnp.stack([z, y, x, k]).astype(jnp.int32)
    block_rows, block_cols = ancestor_inverse.shape
    node_count, _, _ = factor_slots.shape
    panel_rows = block_rows // 32

    split_rows = ancestor_inverse.reshape(4, 4, 2, panel_rows, block_cols)
    leaving = picked(split_rows, 1 - k, 2)
    next_x = step_x(factor_slots, -1)
    last_x = step_x(factor_slots, 1)
    first_piece, leaving, next_x, last_x = lax.optimization_barrier(
        (to_column(factor_slots), leaving, next_x, last_x)
    )
    handed = swap_cores(leaving)
    far_x = hop(
        jnp.where(k == 0, next_x, last_x), lambda z, y, x, k: (z, y, x + 2 * k - 1, k)
    )
    near = [factor_slots, next_x, far_x, last_x]

    behind = []
    ahead = []
    other_behind = []
    other_ahead = []
    moving_up = moving_down = first_piece
    other_first = swap_cores(first_piece)
    for i in range(4):
        if i == 2:
            moving_up, other_first = lax.optimization_barrier((moving_up, other_first))
        if i == 3:
            moving_up, other_behind[0], other_ahead[0], handed, *near = lax.optimization_barrier(
                (moving_up, other_behind[0], other_ahead[0], handed, *near)
            )
        moving_up = step_z(moving_up, 1)
        behind.append(moving_up)
        other_behind.append(swap_cores(moving_up))
        if i < 3:
            moving_down = step_z(moving_down, -1)
            ahead.append(moving_down)
            other_ahead.append(swap_cores(moving_down))
    own_pieces = behind[::-1] + [first_piece] + ahead
    other_pieces = other_behind[::-1] + [other_first] + other_ahead

    def shares(offsets, place):
        return products(
            place, slot_tiles, split_rows, handed, own_pieces, other_pieces, offsets, 0
        )

    middle = shares((2,), place)
    raw = shares((3, 1), after(place, middle[0]))
    own = shares((0,), after(place, raw[0]))
    near[0] = after(near[0], own[0])
    near = stacked(near)
    near_other = swap_cores(near)
    low, high = ring_sum(own, raw[0:2], middle, raw[2:4], step_first)
    low = (lax.optimization_barrier(low[0] + low[1]), low[2])
    high = (lax.optimization_barrier(high[0] + high[1]), high[2])
    here, near, near_other = lax.optimization_barrier((jnp.where(k == 0, y, x), near, near_other))

    def regroup(offset, here):
        at = (here + offset) % 4
        return [sum(picked(share, at, 0) for share in group) for group in (low, high)]

    far = regroup(2, here)
    here, *far = lax.optimization_barrier((here, *far))
    ahead_share, behind_share = regroup(1, here), regroup(3, here)
    here, *raw = lax.optimization_barrier((here, ahead_share[0], behind_share[1]))
    ahead_share[0], behind_share[1] = raw
    own_share = regroup(0, here)
    low, high = ring_sum(own_share, behind_share, far, ahead_share, step_second)
    panels, spread = chain(place, [(low, high)], parent_factor, node_count)

    block_panels = [spread[0]]
    for d in range(1, 4):
        block_panels.append(step_x(spread[d], d))
    keep, send = contraction(place, slot_tiles, block_panels, near, near_other)
    sums = jnp.sum(lax.all_to_all(keep + swap_cores(send), "y", 0, 0, tiled=True), axis=0)
    sums = jnp.sum(lax.all_to_all(sums, "z", 0, 0, tiled=True), axis=0)
    over_z = lax.all_to_all(jnp.broadcast_to(sums, (8,) + sums.shape), "z", 0, 0, tiled=True)
    plane = lax.all_to_all(
        jnp.broadcast_to(over_z, (16,) + over_z.shape), ("y", "x"), 0, 0, tiled=True
    )
    diagonals, parents = tail(place, plane, swap_cores(plane), parent_factor, diag_inverse)
    return panels, diagonals, parents


def solution(mesh):
    grid = Mesh(mesh.devices.reshape(SIZES), AXES)
    placed = (P("z", ("y", "x", "k")), P(None, AXES, None), P(), P(), P())
    return jax.shard_map(
        on_device,
        mesh=grid,
        in_specs=placed,
        out_specs=(P(None, AXES, None), P(), P()),
        check_vma=False,
    )
```
